32 devices in a mesh: cuts: 2 (over y), inter: 16 (over z, x, core).
Axes of the slice: x: 2, y: 2, z: 4, core: 2. Of those that a mesh axis runs over, the one named last changes fastest.
Arguments:
- stem_tensor: bfloat16 [2, 1024, 512, 1, 256], P(None, ('cuts', 'inter')), parts along dimension 1, may hold values from -6 to 6
- branch_one: bfloat16 [2, 512, 512], replicated, may hold values from -0.1875 to 0.1875
- branch_two: bfloat16 [2, 256, 256], replicated, may hold values from -0.25 to 0.25
- mode_order: int32 [256], replicated, may hold values from 0 to 255, each once
- branch_three: bfloat16 [2, 512, 512], replicated, may hold values from -0.1875 to 0.1875
- closing: bfloat16 [2, 512, 512], replicated, may hold values from -4 to 4
Outputs:
- amplitudes: float32 [1024, 512, 2, 1, 256], P(('cuts', 'inter')), parts along dimension 0
The draws below stay inside these ranges and needn't reach their ends.
There are 2 independent parts, one for each index of `cuts`. The reference program is written for one: setup_inputs(seed, part) draws one part's arguments, and reference() takes and returns one part's arrays. A program takes and returns all parts, laid end to end along the dimension named above; an argument that names none is the same for every part. Nothing has to cross between parts.
All inputs are finite; a program needn't handle non-finite values.
Results may differ from the reference program's by a relative error of at most 0.0041.
Values may be sent and summed in bfloat16 or wider, within the bound.
No kernel may reach another device: no remote copies, remote signals or barrier semaphores. Data moves between devices by JAX's collectives and lax.ppermute only.
A program may use at most 192 MiB of HBM per device.

```python
import jax
import jax.numpy as jnp
from jax import lax

SWAP_A = 512
SWAP_B = 512
LOCAL_R = 256
AMPS = 1


def level_of(stream_key, extent, split, low, high):
    level, own = 1.0, jax.random.fold_in(stream_key, 6)
    for dim, parts in split:
        steps = jnp.exp(jax.random.uniform(jax.random.fold_in(own, dim), (parts,), jnp.float32, low / len(split), high / len(split)))
        level = level * jnp.repeat(steps, extent[dim] // parts).reshape([-1 if axis == dim else 1 for axis in range(len(extent))])
    return level


def normal_values(own_key, dims, spread, most, cuts=(), kind=jnp.bfloat16):
    array = jax.random.normal(own_key, dims, jnp.float32) * spread
    if len(cuts) > 0:
        array = level_of(own_key, dims, cuts, -0.22, 0.18) * array
    return jnp.clip(array, min=-most, max=most).astype(kind)


def setup_inputs(seed: int = 0, part: int = 0) -> dict:
    key_list = jax.random.split(jax.random.key(seed), 7)
    part_keys = jax.random.split(jax.random.fold_in(key_list[6], part), 7)
    return {
        "stem_tensor": normal_values(part_keys[0], (2, SWAP_A, SWAP_B, AMPS, LOCAL_R), 1.0, 6.0, ((1, 16),)),
        "branch_one": normal_values(key_list[1], (2, SWAP_A, SWAP_A), (2 * SWAP_A) ** -0.5, 0.1875),
        "branch_two": normal_values(key_list[2], (2, LOCAL_R, LOCAL_R), (2 * LOCAL_R) ** -0.5, 0.25),
        "mode_order": jax.random.permutation(key_list[3], LOCAL_R).astype(jnp.int32),
        "branch_three": normal_values(key_list[4], (2, SWAP_B, SWAP_B), (2 * SWAP_B) ** -0.5, 0.1875),
        "closing": normal_values(key_list[5], (2, SWAP_A, SWAP_B), 0.7, 4.0),
    }


exact_mode = lax.Precision.HIGHEST


def complex_mix(input_real, input_imag, weight_real, weight_imag, pattern):
    def product(first_op, second_op):
        return jnp.einsum(pattern, first_op, second_op, precision=exact_mode)
    return (product(input_real, weight_real) - product(input_imag, weight_imag),
            product(input_real, weight_imag) + product(input_imag, weight_real))


def front_block(block_in, close_block, weights_one, weights_two, mode_order):
    values = block_in.astype(jnp.float32)
    real_part, imag_part = complex_mix(values[0], values[1], weights_one[0], weights_one[1], "abkr,ac->cbkr")
    close_real = close_block[0][:, :, None, None]
    close_imag = close_block[1][:, :, None, None]
    phased = jnp.stack([close_real * real_part - close_imag * imag_part,
                        close_real * imag_part + close_imag * real_part]).astype(jnp.bfloat16)
    reordered = phased.astype(jnp.float32)[..., mode_order]
    real_two, imag_two = complex_mix(reordered[0], reordered[1], weights_two[0], weights_two[1], "abkr,rq->abkq")
    return jnp.stack([real_two, imag_two]).astype(jnp.bfloat16)


def reference(stem_tensor, branch_one, branch_two, mode_order, branch_three, closing):
    weights_one = branch_one.astype(jnp.float32)
    weights_two = branch_two.astype(jnp.float32)
    weights_three = branch_three.astype(jnp.float32)
    close_all = closing.astype(jnp.float32)
    block_cols = 64
    col_blocks = SWAP_B // block_cols

    def front_step(block_index):
        block_in = lax.dynamic_slice_in_dim(stem_tensor, block_index * block_cols, block_cols, 2)
        close_block = lax.dynamic_slice_in_dim(close_all, block_index * block_cols, block_cols, 2)
        return front_block(block_in, close_block, weights_one, weights_two, mode_order)

    pieces = lax.map(front_step, jnp.arange(col_blocks, dtype=jnp.int32))
    second = jnp.moveaxis(pieces, 0, 2).reshape(2, SWAP_A, SWAP_B, AMPS, LOCAL_R)
    block_rows = 16

    def closing_step(block_index):
        row_block = lax.dynamic_slice_in_dim(second, block_index * block_rows, block_rows, 1).astype(jnp.float32)
        out_real, out_imag = complex_mix(row_block[0], row_block[1], weights_three[0], weights_three[1], "abkr,bc->ackr")
        return jnp.stack([out_real, out_imag], axis=2)

    blocks = lax.map(closing_step, jnp.arange(SWAP_A // block_rows, dtype=jnp.int32))
    return blocks.reshape(SWAP_A, SWAP_B, 2, AMPS, LOCAL_R)
```

```python
import functools

import jax
import jax.numpy as jnp
import numpy as np
from jax import lax
from jax.experimental import pallas as pl
from jax.experimental.pallas import tpu as pltpu
from jax.sharding import PartitionSpec as P


B_CHUNKS = 2
A_PARTS = 4
ROWS = 8


def complex_mix(input_real, input_imag, weight_real, weight_imag, pattern):

    def product(first_op, second_op):
        return jnp.einsum(pattern, first_op, second_op, preferred_element_type=jnp.float32)

    return (
        product(input_real, weight_real) - product(input_imag, weight_imag),
        product(input_real, weight_imag) + product(input_imag, weight_real),
    )


def small_blocks(stem_tensor, branch_one, branch_two, mode_order, branch_three, closing):
    group_size = lax.axis_size("inter")
    my_index = lax.axis_index("inter")
    local_b = branch_three.shape[1] // group_size
    permuted = jnp.zeros_like(branch_two).at[:, mode_order, :].set(branch_two)
    close_cols = lax.dynamic_slice_in_dim(closing, my_index * local_b, local_b, 2).astype(
        jnp.float32
    )
    close_real = close_cols[0][:, :, None, None]
    close_imag = close_cols[1][:, :, None, None]
    received = lax.all_to_all(stem_tensor, "inter", split_axis=2, concat_axis=1, tiled=True)
    real_part, imag_part = complex_mix(
        received[0], received[1], branch_one[0], branch_one[1], "abkr,ac->cbkr"
    )
    phased = jnp.stack(
        [
            close_real * real_part - close_imag * imag_part,
            close_real * imag_part + close_imag * real_part,
        ]
    ).astype(jnp.bfloat16)
    real_two, imag_two = complex_mix(
        phased[0], phased[1], permuted[0], permuted[1], "abkr,rq->abkq"
    )
    second = jnp.stack([real_two, imag_two]).astype(jnp.bfloat16)
    returned = lax.all_to_all(second, "inter", split_axis=1, concat_axis=2, tiled=True)
    out_real, out_imag = complex_mix(
        returned[0], returned[1], branch_three[0], branch_three[1], "abkr,bc->ackr"
    )
    return jnp.stack([out_real, out_imag], axis=2)


def rounds_of(group):
    if group % 4:
        return np.array([[(i + k) % group for i in range(group)] for k in range(group)])
    inner = group // 4
    moves = ([1, 3, 0, 2], [2, 0, 3, 1], [3, 2, 1, 0])
    table = [[i for i in range(group)]]
    for move in moves:
        for t in range(inner):
            table.append(
                [move[i // inner] * inner + (i % inner + t) % inner for i in range(group)]
            )
    for t in range(1, inner):
        table.append([i // inner * inner + (i % inner + t) % inner for i in range(group)])
    return np.array(table)


def front_kernel(group, parts, *refs):
    pieces, (w1, w2, close), outs = refs[:group], refs[group : group + 3], refs[group + 3 : -2]
    x, acc = refs[-2:]
    step = pl.program_id(0)
    local_a, width = pieces[0].shape[2:]
    total = group * local_a
    for i, piece in enumerate(pieces):
        for c in range(2):
            x[c * total + i * local_a : c * total + (i + 1) * local_a, :] = piece[c, 0]
    y = jnp.dot(w1[...], x[...], preferred_element_type=jnp.float32)
    lane = lax.broadcasted_iota(jnp.int32, close.shape[1:], 1)

    def column(c):
        return jnp.sum(jnp.where(lane == step, close[c], 0.0), axis=1, keepdims=True)

    cr, ci = column(0), column(1)
    yr, yi = y[:total], y[total:]
    phased = jnp.concatenate(
        [(cr * yr - ci * yi).astype(jnp.bfloat16), (cr * yi + ci * yr).astype(jnp.bfloat16)],
        axis=1,
    )
    both = jnp.dot(phased, w2[...], preferred_element_type=jnp.float32)
    row = lax.rem(step, ROWS)
    for h in range(acc.shape[0]):
        acc[h, pl.ds(row, total, stride=ROWS), :] = both[:, h * 128 : (h + 1) * 128]

    @pl.when(row == ROWS - 1)
    def _():
        count = local_a // parts
        for i in range(group):
            for s in range(parts):
                first = (i * local_a + s * count) * ROWS
                for h in range(acc.shape[0]):
                    c, lanes = divmod(h * 128, width)
                    outs[i * parts + s][c, :, :, lanes : lanes + 128] = (
                        acc[h, first : first + count * ROWS, :]
                        .reshape(count, ROWS, 128)
                        .astype(jnp.bfloat16)
                    )


def front(pieces, w1, w2, close, parts):
    group = len(pieces)
    _, chunk, local_a, width = pieces[0].shape
    total = group * local_a
    count = local_a // parts
    whole = lambda b: (0, 0)
    return pl.pallas_call(
        functools.partial(front_kernel, group, parts),
        grid=(chunk,),
        in_specs=[pl.BlockSpec((2, 1, local_a, width), lambda b: (0, b, 0, 0))] * group
        + [
            pl.BlockSpec(w1.shape, whole),
            pl.BlockSpec(w2.shape, whole),
            pl.BlockSpec(close.shape, lambda b: (0, 0, 0)),
        ],
        out_specs=[pl.BlockSpec((2, count, ROWS, width), lambda b: (0, 0, b // ROWS, 0))]
        * (group * parts),
        out_shape=[jax.ShapeDtypeStruct((2, count, chunk, width), jnp.bfloat16)]
        * (group * parts),
        scratch_shapes=[
            pltpu.VMEM((2 * total, width), jnp.bfloat16),
            pltpu.VMEM((2 * width // 128, total * ROWS, 128), jnp.float32),
        ],
        compiler_params=pltpu.CompilerParams(vmem_limit_bytes=48 << 20),
        name="front",
    )(*pieces, w1, w2, close)


def last_kernel(n_pieces, *refs):
    pieces, w3, out, x = refs[:n_pieces], refs[n_pieces], refs[-2], refs[-1]
    chunk, width = pieces[0].shape[2:]
    total = n_pieces * chunk
    for i, piece in enumerate(pieces):
        for c in range(2):
            x[c * total + i * chunk : c * total + (i + 1) * chunk, :] = piece[c, 0]
    y = jnp.dot(w3[...], x[...], preferred_element_type=jnp.float32)
    split = width // 128
    for h in range(split):
        out[0, pl.ds(h, y.shape[0], stride=split), :] = y[:, h * 128 : (h + 1) * 128]


def last(pieces, w3, base, part, parts):
    _, count, chunk, width = pieces[0].shape
    n = len(pieces)
    rows = w3.shape[0] * (width // 128)
    shape = jax.ShapeDtypeStruct((count * parts, rows, 128), jnp.float32)
    extra = [] if base is None else [base]
    return pl.pallas_call(
        functools.partial(last_kernel, n),
        grid=(count,),
        in_specs=[pl.BlockSpec((2, 1, chunk, width), lambda a: (0, a, 0, 0))] * n
        + [pl.BlockSpec(w3.shape, lambda a: (0, 0))]
        + [pl.BlockSpec(memory_space=pl.ANY)] * len(extra),
        out_specs=pl.BlockSpec((1, rows, 128), lambda a: (a + part * count, 0, 0)),
        out_shape=shape,
        scratch_shapes=[pltpu.VMEM((2 * n * chunk, width), jnp.bfloat16)],
        input_output_aliases={n + 1: 0} if extra else {},
        compiler_params=pltpu.CompilerParams(vmem_limit_bytes=32 << 20),
        name="last",
    )(*pieces, w3, *extra)


def on_device(stem_tensor, branch_one, branch_two, mode_order, branch_three, closing):
    group = lax.axis_size("inter")
    me = lax.axis_index("inter")
    local_a, width = stem_tensor.shape[1], stem_tensor.shape[4]
    size_b = branch_three.shape[1]
    local_b = size_b // group
    chunk = local_b // B_CHUNKS
    size_a = group * local_a
    if (
        local_b % (B_CHUNKS * 2 * ROWS)
        or local_a % (A_PARTS * ROWS)
        or width % 128
        or stem_tensor.shape[3] != 1
    ):
        return small_blocks(stem_tensor, branch_one, branch_two, mode_order, branch_three, closing)

    table = rounds_of(group)
    n_rounds = len(table)
    inverse = np.argsort(table, axis=1)
    target = jnp.asarray(table, jnp.int32)[:, me]
    source = jnp.asarray(inverse, jnp.int32)[:, me]
    pairs = [[(i, int(row[i])) for i in range(group)] for row in table]

    def send(block, k):
        return block if k == 0 else lax.ppermute(block, "inter", pairs[k])

    stem = stem_tensor[:, :, :, 0, :]
    arrived = []
    for j in range(B_CHUNKS):
        got = []
        for k in range(n_rounds):
            block = lax.dynamic_slice_in_dim(stem, target[k] * local_b + j * chunk, chunk, 2)
            got.append(send(jnp.transpose(block, (0, 2, 1, 3)), k))
        arrived.append(got)

    one = branch_one.reshape(2, group, local_a, group, local_a)
    one = one[:, source][:, :, :, target].reshape(2, size_a, size_a)
    one = jnp.transpose(one, (0, 2, 1))
    w1 = jnp.concatenate(
        [
            jnp.concatenate([one[0], -one[1]], axis=1),
            jnp.concatenate([one[1], one[0]], axis=1),
        ],
        axis=0,
    )
    permuted = jnp.zeros_like(branch_two).at[:, mode_order, :].set(branch_two)
    w2 = jnp.concatenate(
        [
            jnp.concatenate([permuted[0], permuted[1]], axis=1),
            jnp.concatenate([-permuted[1], permuted[0]], axis=1),
        ],
        axis=0,
    )
    close = lax.dynamic_slice_in_dim(closing, me * local_b, local_b, 2).astype(jnp.float32)
    close = close.reshape(2, group, local_a, local_b)[:, target].reshape(2, size_a, local_b)
    three = branch_three.reshape(2, group, B_CHUNKS, chunk, size_b)[:, source]
    three = jnp.transpose(three, (0, 4, 2, 1, 3)).reshape(2, size_b, size_b)
    w3 = jnp.stack(
        [
            jnp.concatenate([three[0], -three[1]], axis=1),
            jnp.concatenate([three[1], three[0]], axis=1),
        ],
        axis=1,
    ).reshape(2 * size_b, 2 * size_b)

    returned = [[] for _ in range(A_PARTS)]
    for j in range(B_CHUNKS):
        pieces = front(
            arrived[j], w1, w2, close[:, :, j * chunk : (j + 1) * chunk], A_PARTS
        )
        for s in range(A_PARTS):
            for k in range(n_rounds):
                returned[s].append(send(pieces[k * A_PARTS + s], k))

    out = None
    for s in range(A_PARTS):
        out = last(returned[s], w3, out, s, A_PARTS)
    return out.reshape(local_a, size_b, 2, 1, width)


def solution(mesh):
    in_specs = (P(None, ("cuts", "inter"), None, None, None), P(), P(), P(), P(), P())
    out_specs = P(("cuts", "inter"), None, None, None, None)
    return jax.shard_map(
        on_device, mesh=mesh, in_specs=in_specs, out_specs=out_specs, check_vma=False
    )
```

```python
import functools

import jax
import jax.numpy as jnp
import numpy as np
from jax import lax
from jax.experimental import pallas as pl
from jax.experimental.pallas import tpu as pltpu
from jax.sharding import PartitionSpec as P


B_CHUNKS = 2
LAST_ROWS = 8
ROWS = 8


def complex_mix(input_real, input_imag, weight_real, weight_imag, pattern):

    def product(first_op, second_op):
        return jnp.einsum(pattern, first_op, second_op, preferred_element_type=jnp.float32)

    return (
        product(input_real, weight_real) - product(input_imag, weight_imag),
        product(input_real, weight_imag) + product(input_imag, weight_real),
    )


def small_blocks(stem_tensor, branch_one, branch_two, mode_order, branch_three, closing):
    group_size = lax.axis_size("inter")
    my_index = lax.axis_index("inter")
    local_b = branch_three.shape[1] // group_size
    permuted = jnp.zeros_like(branch_two).at[:, mode_order, :].set(branch_two)
    close_cols = lax.dynamic_slice_in_dim(closing, my_index * local_b, local_b, 2).astype(
        jnp.float32
    )
    close_real = close_cols[0][:, :, None, None]
    close_imag = close_cols[1][:, :, None, None]
    received = lax.all_to_all(stem_tensor, "inter", split_axis=2, concat_axis=1, tiled=True)
    real_part, imag_part = complex_mix(
        received[0], received[1], branch_one[0], branch_one[1], "abkr,ac->cbkr"
    )
    phased = jnp.stack(
        [
            close_real * real_part - close_imag * imag_part,
            close_real * imag_part + close_imag * real_part,
        ]
    ).astype(jnp.bfloat16)
    real_two, imag_two = complex_mix(
        phased[0], phased[1], permuted[0], permuted[1], "abkr,rq->abkq"
    )
    second = jnp.stack([real_two, imag_two]).astype(jnp.bfloat16)
    returned = lax.all_to_all(second, "inter", split_axis=1, concat_axis=2, tiled=True)
    out_real, out_imag = complex_mix(
        returned[0], returned[1], branch_three[0], branch_three[1], "abkr,bc->ackr"
    )
    return jnp.stack([out_real, out_imag], axis=2)


MOVES = ((3, 2, 1, 0), (2, 0, 3, 1), (1, 3, 0, 2))


def rounds_of(group):
    quarters = 4 if group % 4 == 0 else 1
    turns = range(group // quarters)
    moves = MOVES if quarters == 4 else ()
    stay = tuple(range(quarters))
    return [(stay, t) for t in turns] + [(move, t) for move in moves for t in turns]


def inverse_of(rounds, group):
    return [
        (tuple(int(q) for q in np.argsort(move)), -turn % (group // len(move)))
        for move, turn in rounds
    ]


def pairs_of(move, turn, group):
    inner = group // len(move)
    return [
        (i, move[i // inner] * inner + (i % inner + turn) % inner) for i in range(group)
    ]


def partners(index, rounds, group):
    inner = group // len(rounds[0][0])
    quarter, place = index // inner, index % inner
    moved, turned = {}, {}
    for move, turn in rounds:
        if move not in moved:
            steps = [
                jnp.where(quarter == q, jnp.uint32(m * inner), jnp.uint32(0))
                for q, m in enumerate(move)
                if m
            ]
            moved[move] = functools.reduce(jnp.add, steps) if steps else jnp.uint32(0)
        if turn not in turned:
            turned[turn] = (place + jnp.uint32(turn)) % inner
    return [moved[move] + turned[turn] for move, turn in rounds]


def front_kernel(group, splits, *refs):
    pieces, (w1, w2, close), outs = refs[:group], refs[group : group + 3], refs[group + 3 : -2]
    x, acc = refs[-2:]
    step = pl.program_id(0)
    local_a, width = pieces[0].shape[2:]
    total = group * local_a
    for i, piece in enumerate(pieces):
        for c in range(2):
            x[c * total + i * local_a : c * total + (i + 1) * local_a, :] = piece[c, 0]
    y = jnp.dot(w1[...], x[...], preferred_element_type=jnp.float32)
    lane = lax.broadcasted_iota(jnp.int32, close.shape[1:], 1)

    def column(c):
        return jnp.sum(jnp.where(lane == step, close[c], 0.0), axis=1, keepdims=True)

    cr, ci = column(0), column(1)
    yr, yi = y[:total], y[total:]
    phased = jnp.concatenate(
        [(cr * yr - ci * yi).astype(jnp.bfloat16), (cr * yi + ci * yr).astype(jnp.bfloat16)],
        axis=1,
    )
    both = jnp.dot(phased, w2[...], preferred_element_type=jnp.float32)
    row = lax.rem(step, ROWS)
    for h in range(acc.shape[0]):
        acc[h, pl.ds(row, total, stride=ROWS), :] = both[:, h * 128 : (h + 1) * 128]

    @pl.when(row == ROWS - 1)
    def _():
        first = 0
        for i, out in enumerate(outs):
            count = splits[i % len(splits)]
            for h in range(acc.shape[0]):
                c, lanes = divmod(h * 128, width)
                out[c, :, :, lanes : lanes + 128] = (
                    acc[h, first * ROWS : (first + count) * ROWS, :]
                    .reshape(count, ROWS, 128)
                    .astype(jnp.bfloat16)
                )
            first += count


def front(pieces, w1, w2, close, splits):
    group = len(pieces)
    _, chunk, local_a, width = pieces[0].shape
    total = group * local_a
    return pl.pallas_call(
        functools.partial(front_kernel, group, splits),
        grid=(chunk,),
        in_specs=[pl.BlockSpec((2, 1, local_a, width), lambda b: (0, b, 0, 0))] * group
        + [
            pl.BlockSpec(w1.shape, lambda b: (0, 0)),
            pl.BlockSpec(w2.shape, lambda b: (0, 0)),
            pl.BlockSpec(close.shape, lambda b: (0, 0, 0)),
        ],
        out_specs=[
            pl.BlockSpec((2, count, ROWS, width), lambda b: (0, 0, b // ROWS, 0))
            for count in splits
        ]
        * group,
        out_shape=[
            jax.ShapeDtypeStruct((2, count, chunk, width), jnp.bfloat16) for count in splits
        ]
        * group,
        scratch_shapes=[
            pltpu.VMEM((2 * total, width), jnp.bfloat16),
            pltpu.VMEM((2 * width // 128, total * ROWS, 128), jnp.float32),
        ],
        compiler_params=pltpu.CompilerParams(vmem_limit_bytes=48 << 20),
        name="front",
    )(*pieces, w1, w2, close)


def last_kernel(n_pieces, *refs):
    pieces, w3, out, x = refs[:n_pieces], refs[n_pieces], refs[-2], refs[-1]
    chunk, width = pieces[0].shape[2:]
    total = n_pieces * chunk
    for i, piece in enumerate(pieces):
        for c in range(2):
            x[c * total + i * chunk : c * total + (i + 1) * chunk, :] = piece[c, 0]
    y = jnp.dot(w3[...], x[...], preferred_element_type=jnp.float32)
    split = width // 128
    for h in range(split):
        out[0, pl.ds(h, y.shape[0], stride=split), :] = y[:, h * 128 : (h + 1) * 128]


def last(pieces, w3, base, start, count, rows):
    _, _, chunk, width = pieces[0].shape
    n = len(pieces)
    lines = w3.shape[0] * (width // 128)
    extra = [] if base is None else [base]

    def piece_spec(piece):
        skip = 0 if piece.shape[1] == count else start
        return pl.BlockSpec((2, 1, chunk, width), lambda a: (0, a + skip, 0, 0))

    return pl.pallas_call(
        functools.partial(last_kernel, n),
        grid=(count,),
        in_specs=[piece_spec(piece) for piece in pieces]
        + [pl.BlockSpec(w3.shape, lambda a: (0, 0))]
        + [pl.BlockSpec(memory_space=pl.ANY)] * len(extra),
        out_specs=pl.BlockSpec((1, lines, 128), lambda a: (a + start, 0, 0)),
        out_shape=jax.ShapeDtypeStruct((rows, lines, 128), jnp.float32),
        scratch_shapes=[pltpu.VMEM((2 * n * chunk, width), jnp.bfloat16)],
        input_output_aliases={n + 1: 0} if extra else {},
        compiler_params=pltpu.CompilerParams(vmem_limit_bytes=32 << 20),
        name="last",
    )(*[pltpu.with_memory_space_constraint(piece, pltpu.HBM) for piece in pieces], w3, *extra)


def on_device(stem_tensor, branch_one, branch_two, mode_order, branch_three, closing):
    group = lax.axis_size("inter")
    me = lax.axis_index("inter")
    local_a, width = stem_tensor.shape[1], stem_tensor.shape[4]
    size_b = branch_three.shape[1]
    local_b = size_b // group
    chunk = local_b // B_CHUNKS
    size_a = group * local_a
    if (
        local_b % (B_CHUNKS * 2 * ROWS)
        or local_a % ROWS
        or local_a <= LAST_ROWS
        or width % 128
        or stem_tensor.shape[3] != 1
    ):
        return small_blocks(stem_tensor, branch_one, branch_two, mode_order, branch_three, closing)

    rounds = rounds_of(group)
    n_rounds = len(rounds)
    place = me.astype(jnp.uint32)
    zero = jnp.uint32(0)
    target = partners(place, rounds, group)
    pairs = [pairs_of(move, turn, group) for move, turn in rounds]

    def send(block, k):
        return block if k == 0 else lax.ppermute(block, "inter", pairs[k])

    stem = stem_tensor[:, :, :, 0, :]
    arrived = []
    for j in range(B_CHUNKS):
        got = []
        for k in range(n_rounds):
            block = lax.dynamic_slice(
                stem,
                (zero, zero, target[k] * jnp.uint32(local_b) + jnp.uint32(j * chunk), zero),
                (2, local_a, chunk, width),
                allow_negative_indices=False,
            )
            got.append(send(jnp.transpose(block, (0, 2, 1, 3)), k))
        arrived.append(got)

    where_to = jnp.stack(target).astype(jnp.int32)
    where_from = jnp.stack(partners(place, inverse_of(rounds, group), group)).astype(jnp.int32)
    one = branch_one.reshape(2, group, local_a, group, local_a)
    one = one[:, where_from][:, :, :, where_to].reshape(2, size_a, size_a)
    one = jnp.transpose(one, (0, 2, 1))
    w1 = jnp.concatenate(
        [
            jnp.concatenate([one[0], -one[1]], axis=1),
            jnp.concatenate([one[1], one[0]], axis=1),
        ],
        axis=0,
    )
    permuted = jnp.zeros_like(branch_two).at[:, mode_order, :].set(branch_two)
    w2 = jnp.concatenate(
        [
            jnp.concatenate([permuted[0], permuted[1]], axis=1),
            jnp.concatenate([-permuted[1], permuted[0]], axis=1),
        ],
        axis=0,
    )
    close = lax.dynamic_slice_in_dim(closing, me * local_b, local_b, 2).astype(jnp.float32)
    close = close.reshape(2, group, local_a, local_b)[:, where_to].reshape(2, size_a, local_b)
    three = branch_three.reshape(2, group, B_CHUNKS, chunk, size_b)[:, where_from]
    three = jnp.transpose(three, (0, 4, 2, 1, 3)).reshape(2, size_b, size_b)
    w3 = jnp.stack(
        [
            jnp.concatenate([three[0], -three[1]], axis=1),
            jnp.concatenate([three[1], three[0]], axis=1),
        ],
        axis=1,
    ).reshape(2 * size_b, 2 * size_b)
    w1, w2, w3 = lax.optimization_barrier((w1, w2, w3))

    parts = (local_a - LAST_ROWS, LAST_ROWS)
    returned = [[] for _ in parts]
    for j in range(B_CHUNKS):
        splits = parts if j == B_CHUNKS - 1 else (local_a,)
        pieces = front(arrived[j], w1, w2, close[:, :, j * chunk : (j + 1) * chunk], splits)
        for s in range(len(splits)):
            back = [send(pieces[k * len(splits) + s], k) for k in range(n_rounds)]
            for s_to in range(len(parts)) if len(splits) == 1 else (s,):
                returned[s_to] += back

    out, start = None, 0
    for pieces, count in zip(returned, parts):
        out = last(pieces, w3, out, start, count, local_a)
        start += count
    return out.reshape(local_a, size_b, 2, 1, width)


def solution(mesh):
    in_specs = (P(None, ("cuts", "inter"), None, None, None), P(), P(), P(), P(), P())
    out_specs = P(("cuts", "inter"), None, None, None, None)
    return jax.shard_map(
        on_device, mesh=mesh, in_specs=in_specs, out_specs=out_specs, check_vma=False
    )
```

```python
import functools

import jax
import jax.numpy as jnp
import numpy as np
from jax import lax
from jax.experimental import pallas as pl
from jax.experimental.pallas import tpu as pltpu
from jax.sharding import PartitionSpec as P


B_CHUNKS = 2

ROWS = 8
STEP_ROWS = 2


def complex_mix(input_real, input_imag, weight_real, weight_imag, pattern):

    def product(first_op, second_op):
        return jnp.einsum(pattern, first_op, second_op, preferred_element_type=jnp.float32)

    return (
        product(input_real, weight_real) - product(input_imag, weight_imag),
        product(input_real, weight_imag) + product(input_imag, weight_real),
    )


def small_blocks(stem_tensor, branch_one, branch_two, mode_order, branch_three, closing):
    group_size = lax.axis_size("inter")
    my_index = lax.axis_index("inter")
    local_b = branch_three.shape[1] // group_size
    permuted = jnp.zeros_like(branch_two).at[:, mode_order, :].set(branch_two)
    close_cols = lax.dynamic_slice_in_dim(closing, my_index * local_b, local_b, 2).astype(
        jnp.float32
    )
    close_real = close_cols[0][:, :, None, None]
    close_imag = close_cols[1][:, :, None, None]
    received = lax.all_to_all(stem_tensor, "inter", split_axis=2, concat_axis=1, tiled=True)
    real_part, imag_part = complex_mix(
        received[0], received[1], branch_one[0], branch_one[1], "abkr,ac->cbkr"
    )
    phased = jnp.stack(
        [
            close_real * real_part - close_imag * imag_part,
            close_real * imag_part + close_imag * real_part,
        ]
    ).astype(jnp.bfloat16)
    real_two, imag_two = complex_mix(
        phased[0], phased[1], permuted[0], permuted[1], "abkr,rq->abkq"
    )
    second = jnp.stack([real_two, imag_two]).astype(jnp.bfloat16)
    returned = lax.all_to_all(second, "inter", split_axis=1, concat_axis=2, tiled=True)
    out_real, out_imag = complex_mix(
        returned[0], returned[1], branch_three[0], branch_three[1], "abkr,bc->ackr"
    )
    return jnp.stack([out_real, out_imag], axis=2)


MOVES = ((3, 2, 1, 0), (2, 0, 3, 1), (1, 3, 0, 2))


def rounds_of(group):
    quarters = 4 if group % 4 == 0 else 1
    turns = range(group // quarters)
    moves = MOVES if quarters == 4 else ()
    stay = tuple(range(quarters))
    near = [(stay, t) for t in turns]
    far = [(move, t) for move in moves for t in turns]
    return near[:1] + far[:1] + near[1:] + far[1:]


def inverse_of(rounds, group):
    return [
        (tuple(int(q) for q in np.argsort(move)), -turn % (group // len(move)))
        for move, turn in rounds
    ]


def pairs_of(move, turn, group):
    inner = group // len(move)
    return [
        (i, move[i // inner] * inner + (i % inner + turn) % inner) for i in range(group)
    ]


def partners(index, rounds, group):
    inner = group // len(rounds[0][0])
    quarter, place = index // inner, index % inner
    moved, turned = {}, {}
    for move, turn in rounds:
        if move not in moved:
            steps = [
                jnp.where(quarter == q, jnp.uint32(m * inner), jnp.uint32(0))
                for q, m in enumerate(move)
                if m
            ]
            moved[move] = functools.reduce(jnp.add, steps) if steps else jnp.uint32(0)
        if turn not in turned:
            turned[turn] = (place + jnp.uint32(turn)) % inner
    return [moved[move] + turned[turn] for move, turn in rounds]


def front_kernel(group, *refs):
    pieces, (w1, w2, close), outs = refs[:group], refs[group : group + 3], refs[group + 3 : -2]
    x, acc = refs[-2:]
    step = pl.program_id(0)
    local_a, width = pieces[0].shape[2:]
    total = group * local_a
    for i, piece in enumerate(pieces):
        for c in range(2):
            x[c * total + i * local_a : c * total + (i + 1) * local_a, :] = piece[c, 0]
    y = jnp.dot(w1[...], x[...], preferred_element_type=jnp.float32)
    lane = lax.broadcasted_iota(jnp.int32, close.shape[1:], 1)

    def column(c):
        return jnp.sum(jnp.where(lane == step, close[c], 0.0), axis=1, keepdims=True)

    cr, ci = column(0), column(1)
    yr, yi = y[:total], y[total:]
    phased = jnp.concatenate(
        [(cr * yr - ci * yi).astype(jnp.bfloat16), (cr * yi + ci * yr).astype(jnp.bfloat16)],
        axis=1,
    )
    both = jnp.dot(phased, w2[...], preferred_element_type=jnp.float32)
    row = lax.rem(step, ROWS)
    for h in range(acc.shape[0]):
        acc[h, pl.ds(row, total, stride=ROWS), :] = both[:, h * 128 : (h + 1) * 128]

    @pl.when(row == ROWS - 1)
    def _():
        for i, out in enumerate(outs):
            for h in range(acc.shape[0]):
                c, lanes = divmod(h * 128, width)
                out[c, :, :, lanes : lanes + 128] = (
                    acc[h, i * local_a * ROWS : (i + 1) * local_a * ROWS, :]
                    .reshape(local_a, ROWS, 128)
                    .astype(jnp.bfloat16)
                )


def front(pieces, w1, w2, close):
    group = len(pieces)
    _, chunk, local_a, width = pieces[0].shape
    total = group * local_a
    return pl.pallas_call(
        functools.partial(front_kernel, group),
        grid=(chunk,),
        in_specs=[pl.BlockSpec((2, 1, local_a, width), lambda b: (0, b, 0, 0))] * group
        + [
            pl.BlockSpec(w1.shape, lambda b: (0, 0)),
            pl.BlockSpec(w2.shape, lambda b: (0, 0)),
            pl.BlockSpec(close.shape, lambda b: (0, 0, 0)),
        ],
        out_specs=[pl.BlockSpec((2, local_a, ROWS, width), lambda b: (0, 0, b // ROWS, 0))]
        * group,
        out_shape=[jax.ShapeDtypeStruct((2, local_a, chunk, width), jnp.bfloat16)] * group,
        scratch_shapes=[
            pltpu.VMEM((2 * total, width), jnp.bfloat16),
            pltpu.VMEM((2 * width // 128, total * ROWS, 128), jnp.float32),
        ],
        compiler_params=pltpu.CompilerParams(vmem_limit_bytes=40 << 20),
        name="front",
    )(*pieces, w1, w2, close)


def mix_rows(pieces, w3, x, t):
    chunk, _ = pieces[0].shape[2:]
    total = len(pieces) * chunk
    for i, piece in enumerate(pieces):
        for c in range(2):
            x[c * total + i * chunk : c * total + (i + 1) * chunk, :] = piece[c, t]
    return jnp.dot(w3[...], x[...], preferred_element_type=jnp.float32)


def partial_kernel(n, *refs):
    pieces, w3, out, buffers, x, sems = refs[:n], refs[n], *refs[n + 1 :]
    steps = out.shape[0] // STEP_ROWS

    def copies(step, slot):
        rows = pl.ds(step * STEP_ROWS, STEP_ROWS)
        return [
            pltpu.make_async_copy(piece.at[:, rows], buffers.at[slot, i], sems.at[slot, i])
            for i, piece in enumerate(pieces)
        ]

    for copy in copies(0, 0):
        copy.start()

    @pl.loop(0, steps)
    def _(step):
        slot = lax.rem(step, 2)

        @pl.when(step + 1 < steps)
        def _():
            for copy in copies(step + 1, 1 - slot):
                copy.start()

        for copy in copies(step, slot):
            copy.wait()
        held = [buffers.at[slot, i] for i in range(n)]
        for t in range(STEP_ROWS):
            out[step * STEP_ROWS + t] = mix_rows(held, w3, x.at[t], t)


def partial_b(pieces, w3):
    _, local_a, chunk, width = pieces[0].shape
    n = len(pieces)
    return pl.pallas_call(
        functools.partial(partial_kernel, n),
        in_specs=[pl.BlockSpec(memory_space=pl.ANY)] * n
        + [pl.BlockSpec(memory_space=pltpu.VMEM)],
        out_specs=pl.BlockSpec(memory_space=pltpu.VMEM),
        out_shape=jax.ShapeDtypeStruct((local_a, w3.shape[0], width), jnp.float32),
        scratch_shapes=[
            pltpu.VMEM((2, n, 2, STEP_ROWS, chunk, width), jnp.bfloat16),
            pltpu.VMEM((STEP_ROWS, 2 * n * chunk, width), jnp.bfloat16),
            pltpu.SemaphoreType.DMA((2, n)),
        ],
        compiler_params=pltpu.CompilerParams(vmem_limit_bytes=12 << 20),
        name="partial",
    )(*pieces, w3)


def last_kernel(n, *refs):
    pieces, w3, base, out, x = refs[:n], *refs[n:]
    for t in range(out.shape[0]):
        y = base[t] + mix_rows(pieces, w3, x.at[t], t)
        split = y.shape[1] // 128
        for h in range(split):
            out[t, pl.ds(h, y.shape[0], stride=split), :] = y[:, h * 128 : (h + 1) * 128]


def last_b(pieces, w3, base):
    _, local_a, chunk, width = pieces[0].shape
    n = len(pieces)
    lines = w3.shape[0] * (width // 128)
    return pl.pallas_call(
        functools.partial(last_kernel, n),
        grid=(local_a // STEP_ROWS,),
        in_specs=[pl.BlockSpec((2, STEP_ROWS, chunk, width), lambda a: (0, a, 0, 0))] * n
        + [
            pl.BlockSpec(w3.shape, lambda a: (0, 0)),
            pl.BlockSpec((STEP_ROWS,) + base.shape[1:], lambda a: (a, 0, 0)),
        ],
        out_specs=pl.BlockSpec((STEP_ROWS, lines, 128), lambda a: (a, 0, 0)),
        out_shape=jax.ShapeDtypeStruct((local_a, lines, 128), jnp.float32),
        scratch_shapes=[pltpu.VMEM((STEP_ROWS, 2 * n * chunk, width), jnp.bfloat16)],
        compiler_params=pltpu.CompilerParams(vmem_limit_bytes=20 << 20),
        name="last",
    )(*pieces, w3, base)


def on_device(stem_tensor, branch_one, branch_two, mode_order, branch_three, closing):
    group = lax.axis_size("inter")
    me = lax.axis_index("inter")
    local_a, width = stem_tensor.shape[1], stem_tensor.shape[4]
    size_b = branch_three.shape[1]
    local_b = size_b // group
    chunk = local_b // B_CHUNKS
    size_a = group * local_a
    if (
        local_b % (B_CHUNKS * 2 * ROWS)
        or local_a % ROWS
        or width % 128
        or stem_tensor.shape[3] != 1
    ):
        return small_blocks(stem_tensor, branch_one, branch_two, mode_order, branch_three, closing)

    rounds = rounds_of(group)
    n_rounds = len(rounds)
    place = me.astype(jnp.uint32)
    zero = jnp.uint32(0)
    target = partners(place, rounds, group)
    pairs = [pairs_of(move, turn, group) for move, turn in rounds]

    def send(block, k):
        if k == 0:
            return block
        return lax.ppermute(block, "inter", pairs[k])

    stem = stem_tensor[:, :, :, 0, :]
    arrived = []
    for j in range(B_CHUNKS):
        got = []
        for k in range(n_rounds):
            block = lax.dynamic_slice(
                stem,
                (zero, zero, target[k] * jnp.uint32(local_b) + jnp.uint32(j * chunk), zero),
                (2, local_a, chunk, width),
                allow_negative_indices=False,
            )
            got.append(send(jnp.transpose(block, (0, 2, 1, 3)), k))
        arrived.append(got)

    where_to = jnp.stack(target).astype(jnp.int32)
    where_from = jnp.stack(partners(place, inverse_of(rounds, group), group)).astype(jnp.int32)
    one = branch_one.reshape(2, group, local_a, group, local_a)
    one = one[:, where_from][:, :, :, where_to].reshape(2, size_a, size_a)
    one = jnp.transpose(one, (0, 2, 1))
    w1 = jnp.concatenate(
        [
            jnp.concatenate([one[0], -one[1]], axis=1),
            jnp.concatenate([one[1], one[0]], axis=1),
        ],
        axis=0,
    )
    permuted = jnp.zeros_like(branch_two).at[:, mode_order, :].set(branch_two)
    w2 = jnp.concatenate(
        [
            jnp.concatenate([permuted[0], permuted[1]], axis=1),
            jnp.concatenate([-permuted[1], permuted[0]], axis=1),
        ],
        axis=0,
    )
    close = lax.dynamic_slice_in_dim(closing, me * local_b, local_b, 2).astype(jnp.float32)
    close = close.reshape(2, group, local_a, local_b)[:, where_to].reshape(2, size_a, local_b)
    three = branch_three.reshape(2, group, B_CHUNKS, chunk, size_b)[:, where_from]
    three = jnp.transpose(three, (2, 0, 4, 1, 3)).reshape(B_CHUNKS, 2, size_b, group * chunk)
    w3 = [
        jnp.stack(
            [
                jnp.concatenate([part[0], -part[1]], axis=1),
                jnp.concatenate([part[1], part[0]], axis=1),
            ],
            axis=1,
        ).reshape(2 * size_b, 2 * group * chunk)
        for part in three
    ]
    w1, w2, w3 = lax.optimization_barrier((w1, w2, w3))

    returned = []
    for j in range(B_CHUNKS):
        pieces = front(arrived[j], w1, w2, close[:, :, j * chunk : (j + 1) * chunk])
        returned.append([send(piece, k) for k, piece in enumerate(pieces)])

    base = partial_b(returned[0], w3[0])
    out = last_b(returned[1], w3[1], base)
    return out.reshape(local_a, size_b, 2, 1, width)


def solution(mesh):
    in_specs = (P(None, ("cuts", "inter"), None, None, None), P(), P(), P(), P(), P())
    out_specs = P(("cuts", "inter"), None, None, None, None)
    return jax.shard_map(
        on_device, mesh=mesh, in_specs=in_specs, out_specs=out_specs, check_vma=False
    )
```

```python
import functools

import jax
import jax.numpy as jnp
import numpy as np
from jax import lax
from jax.experimental import pallas as pl
from jax.experimental.pallas import tpu as pltpu
from jax.sharding import PartitionSpec as P


B_CHUNKS = 2

ROWS = 8
STEP_ROWS = 2
SUMS = 4


def complex_mix(input_real, input_imag, weight_real, weight_imag, pattern):

    def product(first_op, second_op):
        return jnp.einsum(pattern, first_op, second_op, preferred_element_type=jnp.float32)

    return (
        product(input_real, weight_real) - product(input_imag, weight_imag),
        product(input_real, weight_imag) + product(input_imag, weight_real),
    )


def small_blocks(stem_tensor, branch_one, branch_two, mode_order, branch_three, closing):
    group_size = lax.axis_size("inter")
    my_index = lax.axis_index("inter")
    local_b = branch_three.shape[1] // group_size
    permuted = jnp.zeros_like(branch_two).at[:, mode_order, :].set(branch_two)
    close_cols = lax.dynamic_slice_in_dim(closing, my_index * local_b, local_b, 2).astype(
        jnp.float32
    )
    close_real = close_cols[0][:, :, None, None]
    close_imag = close_cols[1][:, :, None, None]
    received = lax.all_to_all(stem_tensor, "inter", split_axis=2, concat_axis=1, tiled=True)
    real_part, imag_part = complex_mix(
        received[0], received[1], branch_one[0], branch_one[1], "abkr,ac->cbkr"
    )
    phased = jnp.stack(
        [
            close_real * real_part - close_imag * imag_part,
            close_real * imag_part + close_imag * real_part,
        ]
    ).astype(jnp.bfloat16)
    real_two, imag_two = complex_mix(
        phased[0], phased[1], permuted[0], permuted[1], "abkr,rq->abkq"
    )
    second = jnp.stack([real_two, imag_two]).astype(jnp.bfloat16)
    returned = lax.all_to_all(second, "inter", split_axis=1, concat_axis=2, tiled=True)
    out_real, out_imag = complex_mix(
        returned[0], returned[1], branch_three[0], branch_three[1], "abkr,bc->ackr"
    )
    return jnp.stack([out_real, out_imag], axis=2)


MOVES = ((3, 2, 1, 0), (2, 0, 3, 1), (1, 3, 0, 2))


def rounds_of(group):
    quarters = 4 if group % 4 == 0 else 1
    turns = range(group // quarters)
    moves = MOVES if quarters == 4 else ()
    stay = tuple(range(quarters))
    near = [(stay, t) for t in turns]
    far = [(move, t) for move in moves for t in turns]
    return near[:1] + far[:1] + near[1:] + far[1:]


def inverse_of(rounds, group):
    return [
        (tuple(int(q) for q in np.argsort(move)), -turn % (group // len(move)))
        for move, turn in rounds
    ]


def pairs_of(move, turn, group):
    inner = group // len(move)
    return [
        (i, move[i // inner] * inner + (i % inner + turn) % inner) for i in range(group)
    ]


def partners(index, rounds, group):
    inner = group // len(rounds[0][0])
    quarter, place = index // inner, index % inner
    moved, turned = {}, {}
    for move, turn in rounds:
        if move not in moved:
            steps = [
                jnp.where(quarter == q, jnp.uint32(m * inner), jnp.uint32(0))
                for q, m in enumerate(move)
                if m
            ]
            moved[move] = functools.reduce(jnp.add, steps) if steps else jnp.uint32(0)
        if turn not in turned:
            turned[turn] = (place + jnp.uint32(turn)) % inner
    return [moved[move] + turned[turn] for move, turn in rounds]


def front_kernel(group, *refs):
    pieces, (w1, w2, close), outs = refs[:group], refs[group : group + 3], refs[group + 3 : -2]
    x, acc = refs[-2:]
    step = pl.program_id(0)
    local_a, width = pieces[0].shape[2:]
    total = group * local_a
    for i, piece in enumerate(pieces):
        for c in range(2):
            x[c * total + i * local_a : c * total + (i + 1) * local_a, :] = piece[c, 0]
    y = jnp.dot(w1[...], x[...], preferred_element_type=jnp.float32)
    lane = lax.broadcasted_iota(jnp.int32, close.shape[1:], 1)

    def column(c):
        return jnp.sum(jnp.where(lane == step, close[c], 0.0), axis=1, keepdims=True)

    cr, ci = column(0), column(1)
    yr, yi = y[:total], y[total:]
    phased = jnp.concatenate(
        [(cr * yr - ci * yi).astype(jnp.bfloat16), (cr * yi + ci * yr).astype(jnp.bfloat16)],
        axis=1,
    )
    both = jnp.dot(phased, w2[...], preferred_element_type=jnp.float32)
    row = lax.rem(step, ROWS)
    for h in range(acc.shape[0]):
        acc[h, pl.ds(row, total, stride=ROWS), :] = both[:, h * 128 : (h + 1) * 128]

    @pl.when(row == ROWS - 1)
    def _():
        for i, out in enumerate(outs):
            for h in range(acc.shape[0]):
                c, lanes = divmod(h * 128, width)
                out[c, :, :, lanes : lanes + 128] = (
                    acc[h, i * local_a * ROWS : (i + 1) * local_a * ROWS, :]
                    .reshape(local_a, ROWS, 128)
                    .astype(jnp.bfloat16)
                )


def front(pieces, w1, w2, close):
    group = len(pieces)
    _, chunk, local_a, width = pieces[0].shape
    total = group * local_a
    return pl.pallas_call(
        functools.partial(front_kernel, group),
        grid=(chunk,),
        in_specs=[pl.BlockSpec((2, 1, local_a, width), lambda b: (0, b, 0, 0))] * group
        + [
            pl.BlockSpec(w1.shape, lambda b: (0, 0)),
            pl.BlockSpec(w2.shape, lambda b: (0, 0)),
            pl.BlockSpec(close.shape, lambda b: (0, 0, 0)),
        ],
        out_specs=[pl.BlockSpec((2, local_a, ROWS, width), lambda b: (0, 0, b // ROWS, 0))]
        * group,
        out_shape=[pltpu.HBM((2, local_a, chunk, width), jnp.bfloat16)] * group,
        scratch_shapes=[
            pltpu.VMEM((2 * total, width), jnp.bfloat16),
            pltpu.VMEM((2 * width // 128, total * ROWS, 128), jnp.float32),
        ],
        compiler_params=pltpu.CompilerParams(vmem_limit_bytes=40 << 20),
        name="front",
    )(*pieces, w1, w2, close)


def mix_rows(pieces, w3, x, t):
    chunk, _ = pieces[0].shape[2:]
    total = len(pieces) * chunk
    for i, piece in enumerate(pieces):
        for c in range(2):
            x[c * total + i * chunk : c * total + (i + 1) * chunk, :] = piece[c, t]
    return jnp.dot(w3[...], x[...], preferred_element_type=jnp.float32)


def in_steps(pieces, buffers, sems, steps, body):
    def copies(step, slot):
        rows = pl.ds(step * STEP_ROWS, STEP_ROWS)
        return [
            pltpu.make_async_copy(piece.at[:, rows], buffers.at[slot, i], sems.at[slot, i])
            for i, piece in enumerate(pieces)
        ]

    for copy in copies(0, 0):
        copy.start()

    @pl.loop(0, steps)
    def _(step):
        slot = lax.rem(step, 2)

        @pl.when(step + 1 < steps)
        def _():
            for copy in copies(step + 1, 1 - slot):
                copy.start()

        for copy in copies(step, slot):
            copy.wait()
        body(step, [buffers.at[slot, i] for i in range(len(pieces))])


def by_part(row, rows, parts, body):
    for part in range(parts):

        @pl.when((row >= part * rows) & (row < (part + 1) * rows))
        def _():
            body(part, row - part * rows)


def partial_kernel(n, *refs):
    pieces, w3, outs, (buffers, x, sems) = refs[:n], refs[n], refs[n + 1 : -3], refs[-3:]
    rows = outs[0].shape[0]

    def body(step, held):
        for t in range(STEP_ROWS):
            y = mix_rows(held, w3, x.at[t], t)

            def store(part, row):
                outs[part][row] = y

            by_part(step * STEP_ROWS + t, rows, len(outs), store)

    in_steps(pieces, buffers, sems, rows * len(outs) // STEP_ROWS, body)


def last_kernel(n, *refs):
    pieces, w3, bases = refs[:n], refs[n], refs[n + 1 : -6]
    out, buffers, x, held_out, sems, out_sems = refs[-6:]
    rows = bases[0].shape[0]
    steps = rows * len(bases) // STEP_ROWS

    def copy_out(step, slot):
        lines = pl.ds(step * STEP_ROWS, STEP_ROWS)
        return pltpu.make_async_copy(held_out.at[slot], out.at[lines], out_sems.at[slot])

    def body(step, held):
        slot = lax.rem(step, 2)

        @pl.when(step >= 2)
        def _():
            copy_out(step - 2, slot).wait()

        for t in range(STEP_ROWS):
            y = mix_rows(held, w3, x.at[t], t)

            def store(part, row):
                total = bases[part][row] + y
                split = y.shape[1] // 128
                for h in range(split):
                    lines = pl.ds(h, y.shape[0], stride=split)
                    held_out[slot, t, lines, :] = total[:, h * 128 : (h + 1) * 128]

            by_part(step * STEP_ROWS + t, rows, len(bases), store)
        copy_out(step, slot).start()

    in_steps(pieces, buffers, sems, steps, body)
    for step in range(max(steps - 2, 0), steps):
        copy_out(step, step % 2).wait()


def mix_b(pieces, w3, bases=()):
    _, local_a, chunk, width = pieces[0].shape
    n = len(pieces)
    lines = w3.shape[0] * (width // 128)
    scratch = [
        pltpu.VMEM((2, n, 2, STEP_ROWS, chunk, width), jnp.bfloat16),
        pltpu.VMEM((STEP_ROWS, 2 * n * chunk, width), jnp.bfloat16),
    ]
    sems = [pltpu.SemaphoreType.DMA((2, n))]
    vmem = pl.BlockSpec(memory_space=pltpu.VMEM)
    hbm = pl.BlockSpec(memory_space=pl.ANY)
    if bases:
        scratch += [pltpu.VMEM((2, STEP_ROWS, lines, 128), jnp.float32)]
        sems += [pltpu.SemaphoreType.DMA((2,))]
        bases = [pltpu.with_memory_space_constraint(base, pltpu.VMEM) for base in bases]
        shape, out_specs = jax.ShapeDtypeStruct((local_a, lines, 128), jnp.float32), hbm
    else:
        part = pltpu.VMEM((local_a // SUMS, w3.shape[0], width), jnp.float32)
        shape, out_specs = [part] * SUMS, [vmem] * SUMS
    return pl.pallas_call(
        functools.partial(last_kernel if bases else partial_kernel, n),
        in_specs=[hbm] * n + [vmem] * (1 + len(bases)),
        out_specs=out_specs,
        out_shape=shape,
        scratch_shapes=scratch + sems,
        compiler_params=pltpu.CompilerParams(vmem_limit_bytes=12 << 20),
        name="last" if bases else "partial",
    )(
        *[pltpu.with_memory_space_constraint(piece, pltpu.HBM) for piece in pieces],
        w3,
        *bases,
    )


def on_device(stem_tensor, branch_one, branch_two, mode_order, branch_three, closing):
    group = lax.axis_size("inter")
    me = lax.axis_index("inter")
    local_a, width = stem_tensor.shape[1], stem_tensor.shape[4]
    size_b = branch_three.shape[1]
    local_b = size_b // group
    chunk = local_b // B_CHUNKS
    size_a = group * local_a
    if (
        local_b % (B_CHUNKS * 2 * ROWS)
        or local_a % ROWS
        or local_a % (SUMS * STEP_ROWS)
        or width % 128
        or stem_tensor.shape[3] != 1
    ):
        return small_blocks(stem_tensor, branch_one, branch_two, mode_order, branch_three, closing)

    rounds = rounds_of(group)
    n_rounds = len(rounds)
    place = me.astype(jnp.uint32)
    zero = jnp.uint32(0)
    target = partners(place, rounds, group)
    pairs = [pairs_of(move, turn, group) for move, turn in rounds]

    def send(block, k):
        if k == 0:
            return block
        return lax.ppermute(block, "inter", pairs[k])

    stem = stem_tensor[:, :, :, 0, :]
    arrived = []
    for j in range(B_CHUNKS):
        got = []
        for k in range(n_rounds):
            block = lax.dynamic_slice(
                stem,
                (zero, zero, target[k] * jnp.uint32(local_b) + jnp.uint32(j * chunk), zero),
                (2, local_a, chunk, width),
                allow_negative_indices=False,
            )
            got.append(send(jnp.transpose(block, (0, 2, 1, 3)), k))
        arrived.append(got)

    where_to = jnp.stack(target).astype(jnp.int32)
    where_from = jnp.stack(partners(place, inverse_of(rounds, group), group)).astype(jnp.int32)
    one = branch_one.reshape(2, group, local_a, group, local_a)
    one = one[:, where_from][:, :, :, where_to].reshape(2, size_a, size_a)
    one = jnp.transpose(one, (0, 2, 1))
    w1 = jnp.concatenate(
        [
            jnp.concatenate([one[0], -one[1]], axis=1),
            jnp.concatenate([one[1], one[0]], axis=1),
        ],
        axis=0,
    )
    permuted = jnp.zeros_like(branch_two).at[:, mode_order, :].set(branch_two)
    w2 = jnp.concatenate(
        [
            jnp.concatenate([permuted[0], permuted[1]], axis=1),
            jnp.concatenate([-permuted[1], permuted[0]], axis=1),
        ],
        axis=0,
    )
    close = lax.dynamic_slice_in_dim(closing, me * local_b, local_b, 2).astype(jnp.float32)
    close = close.reshape(2, group, local_a, local_b)[:, where_to].reshape(2, size_a, local_b)
    three = branch_three.reshape(2, group, B_CHUNKS, chunk, size_b)[:, where_from]
    three = jnp.transpose(three, (2, 0, 4, 1, 3)).reshape(B_CHUNKS, 2, size_b, group * chunk)
    w3 = [
        jnp.stack(
            [
                jnp.concatenate([part[0], -part[1]], axis=1),
                jnp.concatenate([part[1], part[0]], axis=1),
            ],
            axis=1,
        ).reshape(2 * size_b, 2 * group * chunk)
        for part in three
    ]
    w1, w2, w3 = lax.optimization_barrier((w1, w2, w3))

    returned = []
    for j in range(B_CHUNKS):
        pieces = front(arrived[j], w1, w2, close[:, :, j * chunk : (j + 1) * chunk])
        returned.append([send(piece, k) for k, piece in enumerate(pieces)])

    sums = mix_b(returned[0], w3[0])
    out = mix_b(returned[1], w3[1], sums)
    return out.reshape(local_a, size_b, 2, 1, width)


def solution(mesh):
    in_specs = (P(None, ("cuts", "inter"), None, None, None), P(), P(), P(), P(), P())
    out_specs = P(("cuts", "inter"), None, None, None, None)
    return jax.shard_map(
        on_device, mesh=mesh, in_specs=in_specs, out_specs=out_specs, check_vma=False
    )
```

```python
import functools

import jax
import jax.numpy as jnp
import numpy as np
from jax import lax
from jax.experimental import pallas as pl
from jax.experimental.pallas import tpu as pltpu
from jax.sharding import PartitionSpec as P


B_CHUNKS = 2

ROWS = 8
STEP_ROWS = 2
SUM_ROWS = 8
LAST_ROWS = 8


def complex_mix(input_real, input_imag, weight_real, weight_imag, pattern):

    def product(first_op, second_op):
        return jnp.einsum(pattern, first_op, second_op, preferred_element_type=jnp.float32)

    return (
        product(input_real, weight_real) - product(input_imag, weight_imag),
        product(input_real, weight_imag) + product(input_imag, weight_real),
    )


def small_blocks(stem_tensor, branch_one, branch_two, mode_order, branch_three, closing):
    group_size = lax.axis_size("inter")
    my_index = lax.axis_index("inter")
    local_b = branch_three.shape[1] // group_size
    permuted = jnp.zeros_like(branch_two).at[:, mode_order, :].set(branch_two)
    close_cols = lax.dynamic_slice_in_dim(closing, my_index * local_b, local_b, 2).astype(
        jnp.float32
    )
    close_real = close_cols[0][:, :, None, None]
    close_imag = close_cols[1][:, :, None, None]
    received = lax.all_to_all(stem_tensor, "inter", split_axis=2, concat_axis=1, tiled=True)
    real_part, imag_part = complex_mix(
        received[0], received[1], branch_one[0], branch_one[1], "abkr,ac->cbkr"
    )
    phased = jnp.stack(
        [
            close_real * real_part - close_imag * imag_part,
            close_real * imag_part + close_imag * real_part,
        ]
    ).astype(jnp.bfloat16)
    real_two, imag_two = complex_mix(
        phased[0], phased[1], permuted[0], permuted[1], "abkr,rq->abkq"
    )
    second = jnp.stack([real_two, imag_two]).astype(jnp.bfloat16)
    returned = lax.all_to_all(second, "inter", split_axis=1, concat_axis=2, tiled=True)
    out_real, out_imag = complex_mix(
        returned[0], returned[1], branch_three[0], branch_three[1], "abkr,bc->ackr"
    )
    return jnp.stack([out_real, out_imag], axis=2)


MOVES = ((3, 2, 1, 0), (2, 0, 3, 1), (1, 3, 0, 2))


def rounds_of(group):
    quarters = 4 if group % 4 == 0 else 1
    turns = range(group // quarters)
    moves = MOVES if quarters == 4 else ()
    stay = tuple(range(quarters))
    near = [(stay, t) for t in turns]
    far = [(move, t) for move in moves for t in turns]
    return near[:1] + far[:1] + near[1:] + far[1:]


def inverse_of(rounds, group):
    return [
        (tuple(int(q) for q in np.argsort(move)), -turn % (group // len(move)))
        for move, turn in rounds
    ]


def pairs_of(move, turn, group):
    inner = group // len(move)
    return [
        (i, move[i // inner] * inner + (i % inner + turn) % inner) for i in range(group)
    ]


def partners(index, rounds, group):
    inner = group // len(rounds[0][0])
    quarter, place = index // inner, index % inner
    moved, turned = {}, {}
    for move, turn in rounds:
        if move not in moved:
            steps = [
                jnp.where(quarter == q, jnp.uint32(m * inner), jnp.uint32(0))
                for q, m in enumerate(move)
                if m
            ]
            moved[move] = functools.reduce(jnp.add, steps) if steps else jnp.uint32(0)
        if turn not in turned:
            turned[turn] = (place + jnp.uint32(turn)) % inner
    return [moved[move] + turned[turn] for move, turn in rounds]


def front_kernel(group, splits, *refs):
    pieces, (w1, w2, close), outs = refs[:group], refs[group : group + 3], refs[group + 3 : -2]
    x, acc = refs[-2:]
    step = pl.program_id(0)
    local_a, width = pieces[0].shape[2:]
    total = group * local_a
    for i, piece in enumerate(pieces):
        for c in range(2):
            x[c * total + i * local_a : c * total + (i + 1) * local_a, :] = piece[c, 0]
    y = jnp.dot(w1[...], x[...], preferred_element_type=jnp.float32)
    lane = lax.broadcasted_iota(jnp.int32, close.shape[1:], 1)

    def column(c):
        return jnp.sum(jnp.where(lane == step, close[c], 0.0), axis=1, keepdims=True)

    cr, ci = column(0), column(1)
    yr, yi = y[:total], y[total:]
    phased = jnp.concatenate(
        [(cr * yr - ci * yi).astype(jnp.bfloat16), (cr * yi + ci * yr).astype(jnp.bfloat16)],
        axis=1,
    )
    both = jnp.dot(phased, w2[...], preferred_element_type=jnp.float32)
    row = lax.rem(step, ROWS)
    for h in range(acc.shape[0]):
        acc[h, pl.ds(row, total, stride=ROWS), :] = both[:, h * 128 : (h + 1) * 128]

    @pl.when(row == ROWS - 1)
    def _():
        first = 0
        for i, out in enumerate(outs):
            count = splits[i % len(splits)]
            for h in range(acc.shape[0]):
                c, lanes = divmod(h * 128, width)
                out[c, :, :, lanes : lanes + 128] = (
                    acc[h, first * ROWS : (first + count) * ROWS, :]
                    .reshape(count, ROWS, 128)
                    .astype(jnp.bfloat16)
                )
            first += count


def front(pieces, w1, w2, close, splits):
    group = len(pieces)
    _, chunk, local_a, width = pieces[0].shape
    total = group * local_a
    return pl.pallas_call(
        functools.partial(front_kernel, group, splits),
        grid=(chunk,),
        in_specs=[pl.BlockSpec((2, 1, local_a, width), lambda b: (0, b, 0, 0))] * group
        + [
            pl.BlockSpec(w1.shape, lambda b: (0, 0)),
            pl.BlockSpec(w2.shape, lambda b: (0, 0)),
            pl.BlockSpec(close.shape, lambda b: (0, 0, 0)),
        ],
        out_specs=[
            pl.BlockSpec((2, count, ROWS, width), lambda b: (0, 0, b // ROWS, 0))
            for count in splits
        ]
        * group,
        out_shape=[pltpu.HBM((2, count, chunk, width), jnp.bfloat16) for count in splits] * group,
        scratch_shapes=[
            pltpu.VMEM((2 * total, width), jnp.bfloat16),
            pltpu.VMEM((2 * width // 128, total * ROWS, 128), jnp.float32),
        ],
        compiler_params=pltpu.CompilerParams(vmem_limit_bytes=40 << 20),
        name="front",
    )(*pieces, w1, w2, close)


def mix_rows(pieces, w3, x, t):
    chunk, _ = pieces[0].shape[2:]
    total = len(pieces) * chunk
    for i, piece in enumerate(pieces):
        for c in range(2):
            x[c * total + i * chunk : c * total + (i + 1) * chunk, :] = piece[c, t]
    return jnp.dot(w3[...], x[...], preferred_element_type=jnp.float32)


def in_steps(pieces, buffers, sems, parts, steps, body):
    def copies(step, slot):
        rows = pl.ds(step * STEP_ROWS, STEP_ROWS)
        return [
            pltpu.make_async_copy(piece.at[:, rows], buffers.at[slot, i], sems.at[slot, i])
            for i, piece in enumerate(pieces)
        ]

    for copy in copies(0, 0):
        copy.start()
    for part in range(parts):

        @pl.loop(0, steps)
        def _(own):
            step = part * steps + own
            slot = lax.rem(step, 2)

            @pl.when(step + 1 < parts * steps)
            def _():
                for copy in copies(step + 1, 1 - slot):
                    copy.start()

            for copy in copies(step, slot):
                copy.wait()
            body(part, own, step, [buffers.at[slot, i] for i in range(len(pieces))])


def partial_kernel(n, *refs):
    pieces, w3, outs, (buffers, x, sems) = refs[:n], refs[n], refs[n + 1 : -3], refs[-3:]

    def body(part, own, step, held):
        for t in range(STEP_ROWS):
            outs[part][own * STEP_ROWS + t] = mix_rows(held, w3, x.at[t], t)

    in_steps(pieces, buffers, sems, len(outs), outs[0].shape[0] // STEP_ROWS, body)


def last_kernel(n, n_bases, start, *refs):
    pieces, w3, bases = refs[:n], refs[n], refs[n + 1 : n + 1 + n_bases]
    out, buffers, x, held_out, sems, out_sems = refs[-6:]
    part_steps = bases[0].shape[0] // STEP_ROWS
    steps = part_steps * n_bases

    def copy_out(step, slot):
        rows = pl.ds(start + step * STEP_ROWS, STEP_ROWS)
        return pltpu.make_async_copy(held_out.at[slot], out.at[rows], out_sems.at[slot])

    def body(part, own, step, held):
        slot = lax.rem(step, 2)

        @pl.when(step >= 2)
        def _():
            copy_out(step - 2, slot).wait()

        for t in range(STEP_ROWS):
            y = bases[part][own * STEP_ROWS + t] + mix_rows(held, w3, x.at[t], t)
            split = y.shape[1] // 128
            for h in range(split):
                lines = pl.ds(h, y.shape[0], stride=split)
                held_out[slot, t, lines, :] = y[:, h * 128 : (h + 1) * 128]
        copy_out(step, slot).start()

    in_steps(pieces, buffers, sems, n_bases, part_steps, body)
    for step in range(max(steps - 2, 0), steps):
        copy_out(step, step % 2).wait()


def in_hbm(pieces):
    return [pltpu.with_memory_space_constraint(piece, pltpu.HBM) for piece in pieces]


def scratch_of(pieces):
    n, (_, _, chunk, width) = len(pieces), pieces[0].shape
    return [
        pltpu.VMEM((2, n, 2, STEP_ROWS, chunk, width), jnp.bfloat16),
        pltpu.VMEM((STEP_ROWS, 2 * n * chunk, width), jnp.bfloat16),
    ]


def partial_b(pieces, w3):
    _, local_a, _, width = pieces[0].shape
    n, count = len(pieces), local_a // SUM_ROWS
    vmem = pl.BlockSpec(memory_space=pltpu.VMEM)
    return pl.pallas_call(
        functools.partial(partial_kernel, n),
        in_specs=[pl.BlockSpec(memory_space=pl.ANY)] * n + [vmem],
        out_specs=[vmem] * count,
        out_shape=[pltpu.VMEM((SUM_ROWS, w3.shape[0], width), jnp.float32)] * count,
        scratch_shapes=scratch_of(pieces) + [pltpu.SemaphoreType.DMA((2, n))],
        compiler_params=pltpu.CompilerParams(vmem_limit_bytes=12 << 20),
        name="partial",
    )(*in_hbm(pieces), w3)


def last_b(pieces, w3, bases, out, start, rows):
    width = pieces[0].shape[3]
    n, lines = len(pieces), w3.shape[0] * (width // 128)
    vmem = pl.BlockSpec(memory_space=pltpu.VMEM)
    any_space = pl.BlockSpec(memory_space=pl.ANY)
    given = [] if out is None else [out]
    return pl.pallas_call(
        functools.partial(last_kernel, n, len(bases), start),
        in_specs=[any_space] * n + [vmem] * (1 + len(bases)) + [any_space] * len(given),
        out_specs=any_space,
        out_shape=jax.ShapeDtypeStruct((rows, lines, 128), jnp.float32),
        input_output_aliases={n + 1 + len(bases): 0} if given else {},
        scratch_shapes=scratch_of(pieces)
        + [
            pltpu.VMEM((2, STEP_ROWS, lines, 128), jnp.float32),
            pltpu.SemaphoreType.DMA((2, n)),
            pltpu.SemaphoreType.DMA((2,)),
        ],
        compiler_params=pltpu.CompilerParams(vmem_limit_bytes=12 << 20),
        name="last",
    )(
        *in_hbm(pieces),
        w3,
        *[pltpu.with_memory_space_constraint(base, pltpu.VMEM) for base in bases],
        *given,
    )


def on_device(stem_tensor, branch_one, branch_two, mode_order, branch_three, closing):
    group = lax.axis_size("inter")
    me = lax.axis_index("inter")
    local_a, width = stem_tensor.shape[1], stem_tensor.shape[4]
    size_b = branch_three.shape[1]
    local_b = size_b // group
    chunk = local_b // B_CHUNKS
    size_a = group * local_a
    if (
        local_b % (B_CHUNKS * 2 * ROWS)
        or local_a % ROWS
        or local_a % SUM_ROWS
        or local_a <= LAST_ROWS
        or width % 128
        or stem_tensor.shape[3] != 1
    ):
        return small_blocks(stem_tensor, branch_one, branch_two, mode_order, branch_three, closing)

    rounds = rounds_of(group)
    n_rounds = len(rounds)
    place = me.astype(jnp.uint32)
    zero = jnp.uint32(0)
    target = partners(place, rounds, group)
    pairs = [pairs_of(move, turn, group) for move, turn in rounds]

    def send(block, k):
        if k == 0:
            return block
        return lax.ppermute(block, "inter", pairs[k])

    stem = stem_tensor[:, :, :, 0, :]
    arrived = []
    for j in range(B_CHUNKS):
        got = []
        for k in range(n_rounds):
            block = lax.dynamic_slice(
                stem,
                (zero, zero, target[k] * jnp.uint32(local_b) + jnp.uint32(j * chunk), zero),
                (2, local_a, chunk, width),
                allow_negative_indices=False,
            )
            got.append(send(jnp.transpose(block, (0, 2, 1, 3)), k))
        arrived.append(got)

    where_to = jnp.stack(target).astype(jnp.int32)
    where_from = jnp.stack(partners(place, inverse_of(rounds, group), group)).astype(jnp.int32)
    one = branch_one.reshape(2, group, local_a, group, local_a)
    one = one[:, where_from][:, :, :, where_to].reshape(2, size_a, size_a)
    one = jnp.transpose(one, (0, 2, 1))
    w1 = jnp.concatenate(
        [
            jnp.concatenate([one[0], -one[1]], axis=1),
            jnp.concatenate([one[1], one[0]], axis=1),
        ],
        axis=0,
    )
    permuted = jnp.zeros_like(branch_two).at[:, mode_order, :].set(branch_two)
    w2 = jnp.concatenate(
        [
            jnp.concatenate([permuted[0], permuted[1]], axis=1),
            jnp.concatenate([-permuted[1], permuted[0]], axis=1),
        ],
        axis=0,
    )
    close = lax.dynamic_slice_in_dim(closing, me * local_b, local_b, 2).astype(jnp.float32)
    close = close.reshape(2, group, local_a, local_b)[:, where_to].reshape(2, size_a, local_b)
    three = branch_three.reshape(2, group, B_CHUNKS, chunk, size_b)[:, where_from]
    three = jnp.transpose(three, (2, 0, 4, 1, 3)).reshape(B_CHUNKS, 2, size_b, group * chunk)
    w3 = [
        jnp.stack(
            [
                jnp.concatenate([part[0], -part[1]], axis=1),
                jnp.concatenate([part[1], part[0]], axis=1),
            ],
            axis=1,
        ).reshape(2 * size_b, 2 * group * chunk)
        for part in three
    ]
    w1, w2, w3 = lax.optimization_barrier((w1, w2, w3))

    returned = []
    parts = (local_a - LAST_ROWS, LAST_ROWS)
    for j in range(B_CHUNKS):
        splits = parts if j else (local_a,)
        pieces = front(arrived[j], w1, w2, close[:, :, j * chunk : (j + 1) * chunk], splits)
        for i in range(len(splits)):
            returned.append([send(piece, k) for k, piece in enumerate(pieces[i :: len(splits)])])

    sums = partial_b(returned[0], w3[0])
    out, start = None, 0
    for i, count in enumerate(parts):
        own = sums[start // SUM_ROWS : (start + count) // SUM_ROWS]
        out = last_b(returned[1 + i], w3[1], own, out, start, local_a)
        start += count
    return out.reshape(local_a, size_b, 2, 1, width)


def solution(mesh):
    in_specs = (P(None, ("cuts", "inter"), None, None, None), P(), P(), P(), P(), P())
    out_specs = P(("cuts", "inter"), None, None, None, None)
    return jax.shard_map(
        on_device, mesh=mesh, in_specs=in_specs, out_specs=out_specs, check_vma=False
    )
```

```python
import functools

import jax
import jax.numpy as jnp
import numpy as np
from jax import lax
from jax.experimental import pallas as pl
from jax.experimental.pallas import tpu as pltpu
from jax.sharding import PartitionSpec as P


B_CHUNKS = 2

ROWS = 8
STEP_ROWS = 2
SUM_ROWS = 8
LAST_ROWS = 8


def complex_mix(input_real, input_imag, weight_real, weight_imag, pattern):

    def product(first_op, second_op):
        return jnp.einsum(pattern, first_op, second_op, preferred_element_type=jnp.float32)

    return (
        product(input_real, weight_real) - product(input_imag, weight_imag),
        product(input_real, weight_imag) + product(input_imag, weight_real),
    )


def small_blocks(stem_tensor, branch_one, branch_two, mode_order, branch_three, closing):
    group_size = lax.axis_size("inter")
    my_index = lax.axis_index("inter")
    local_b = branch_three.shape[1] // group_size
    permuted = jnp.zeros_like(branch_two).at[:, mode_order, :].set(branch_two)
    close_cols = lax.dynamic_slice_in_dim(closing, my_index * local_b, local_b, 2).astype(
        jnp.float32
    )
    close_real = close_cols[0][:, :, None, None]
    close_imag = close_cols[1][:, :, None, None]
    received = lax.all_to_all(stem_tensor, "inter", split_axis=2, concat_axis=1, tiled=True)
    real_part, imag_part = complex_mix(
        received[0], received[1], branch_one[0], branch_one[1], "abkr,ac->cbkr"
    )
    phased = jnp.stack(
        [
            close_real * real_part - close_imag * imag_part,
            close_real * imag_part + close_imag * real_part,
        ]
    ).astype(jnp.bfloat16)
    real_two, imag_two = complex_mix(
        phased[0], phased[1], permuted[0], permuted[1], "abkr,rq->abkq"
    )
    second = jnp.stack([real_two, imag_two]).astype(jnp.bfloat16)
    returned = lax.all_to_all(second, "inter", split_axis=1, concat_axis=2, tiled=True)
    out_real, out_imag = complex_mix(
        returned[0], returned[1], branch_three[0], branch_three[1], "abkr,bc->ackr"
    )
    return jnp.stack([out_real, out_imag], axis=2)


MOVES = ((3, 2, 1, 0), (2, 0, 3, 1), (1, 3, 0, 2))


def rounds_of(group):
    quarters = 4 if group % 4 == 0 else 1
    turns = range(group // quarters)
    moves = MOVES if quarters == 4 else ()
    stay = tuple(range(quarters))
    near = [(stay, t) for t in turns]
    far = [(move, t) for move in moves for t in turns]
    return near[:1] + far[:1] + near[1:] + far[1:]


def inverse_of(rounds, group):
    return [
        (tuple(int(q) for q in np.argsort(move)), -turn % (group // len(move)))
        for move, turn in rounds
    ]


def pairs_of(move, turn, group):
    inner = group // len(move)
    return [
        (i, move[i // inner] * inner + (i % inner + turn) % inner) for i in range(group)
    ]


def partners(index, rounds, group):
    inner = group // len(rounds[0][0])
    quarter, place = index // inner, index % inner
    moved, turned = {}, {}
    for move, turn in rounds:
        if move not in moved:
            steps = [
                jnp.where(quarter == q, jnp.uint32(m * inner), jnp.uint32(0))
                for q, m in enumerate(move)
                if m
            ]
            moved[move] = functools.reduce(jnp.add, steps) if steps else jnp.uint32(0)
        if turn not in turned:
            turned[turn] = (place + jnp.uint32(turn)) % inner
    return [moved[move] + turned[turn] for move, turn in rounds]


def front_kernel(group, splits, *refs):
    pieces, (w1, w2, close), outs = refs[:group], refs[group : group + 3], refs[group + 3 : -2]
    x, acc = refs[-2:]
    step = pl.program_id(0)
    local_a, width = pieces[0].shape[2:]
    total = group * local_a
    for i, piece in enumerate(pieces):
        for c in range(2):
            x[c * total + i * local_a : c * total + (i + 1) * local_a, :] = piece[c, 0]
    y = jnp.dot(w1[...], x[...], preferred_element_type=jnp.float32)
    lane = lax.broadcasted_iota(jnp.int32, close.shape[1:], 1)

    def column(c):
        return jnp.sum(jnp.where(lane == step, close[c], 0.0), axis=1, keepdims=True)

    cr, ci = column(0), column(1)
    yr, yi = y[:total], y[total:]
    phased = jnp.concatenate(
        [(cr * yr - ci * yi).astype(jnp.bfloat16), (cr * yi + ci * yr).astype(jnp.bfloat16)],
        axis=1,
    )
    both = jnp.dot(phased, w2[...], preferred_element_type=jnp.float32)
    row = lax.rem(step, ROWS)
    for h in range(acc.shape[0]):
        acc[h, pl.ds(row, total, stride=ROWS), :] = both[:, h * 128 : (h + 1) * 128]

    @pl.when(row == ROWS - 1)
    def _():
        first = 0
        for i, out in enumerate(outs):
            count = splits[i % len(splits)]
            for h in range(acc.shape[0]):
                c, lanes = divmod(h * 128, width)
                out[c, :, :, lanes : lanes + 128] = (
                    acc[h, first * ROWS : (first + count) * ROWS, :]
                    .reshape(count, ROWS, 128)
                    .astype(jnp.bfloat16)
                )
            first += count


def front(pieces, w1, w2, close, splits):
    group = len(pieces)
    _, chunk, local_a, width = pieces[0].shape
    total = group * local_a
    return pl.pallas_call(
        functools.partial(front_kernel, group, splits),
        grid=(chunk,),
        in_specs=[pl.BlockSpec((2, 1, local_a, width), lambda b: (0, b, 0, 0))] * group
        + [
            pl.BlockSpec(w1.shape, lambda b: (0, 0)),
            pl.BlockSpec(w2.shape, lambda b: (0, 0)),
            pl.BlockSpec(close.shape, lambda b: (0, 0, 0)),
        ],
        out_specs=[
            pl.BlockSpec((2, count, ROWS, width), lambda b: (0, 0, b // ROWS, 0))
            for count in splits
        ]
        * group,
        out_shape=[pltpu.HBM((2, count, chunk, width), jnp.bfloat16) for count in splits] * group,
        scratch_shapes=[
            pltpu.VMEM((2 * total, width), jnp.bfloat16),
            pltpu.VMEM((2 * width // 128, total * ROWS, 128), jnp.float32),
        ],
        compiler_params=pltpu.CompilerParams(vmem_limit_bytes=40 << 20),
        name="front",
    )(*pieces, w1, w2, close)


def mix_rows(pieces, w3, x, t):
    chunk, _ = pieces[0].shape[2:]
    total = len(pieces) * chunk
    for i, piece in enumerate(pieces):
        for c in range(2):
            x[c * total + i * chunk : c * total + (i + 1) * chunk, :] = piece[c, t]
    return jnp.dot(w3[...], x[...], preferred_element_type=jnp.float32)


def in_place(pieces, parts, steps, body):
    for part in range(parts):

        @pl.loop(0, steps)
        def _(own):
            step = part * steps + own
            rows = pl.ds(step * STEP_ROWS, STEP_ROWS)
            body(part, own, step, [piece.at[:, rows] for piece in pieces])


def in_steps(pieces, buffers, sems, parts, steps, body):
    def copies(step, slot):
        rows = pl.ds(step * STEP_ROWS, STEP_ROWS)
        return [
            pltpu.make_async_copy(piece.at[:, rows], buffers.at[slot, i], sems.at[slot, i])
            for i, piece in enumerate(pieces)
        ]

    for copy in copies(0, 0):
        copy.start()
    for part in range(parts):

        @pl.loop(0, steps)
        def _(own):
            step = part * steps + own
            slot = lax.rem(step, 2)

            @pl.when(step + 1 < parts * steps)
            def _():
                for copy in copies(step + 1, 1 - slot):
                    copy.start()

            for copy in copies(step, slot):
                copy.wait()
            body(part, own, step, [buffers.at[slot, i] for i in range(len(pieces))])


def partial_kernel(n, *refs):
    pieces, w3, outs, (x, buffers, sems) = refs[:n], refs[n], refs[n + 1 : -3], refs[-3:]

    def body(part, own, step, held):
        for t in range(STEP_ROWS):
            outs[part][own * STEP_ROWS + t] = mix_rows(held, w3, x.at[t], t)

    in_steps(pieces, buffers, sems, len(outs), outs[0].shape[0] // STEP_ROWS, body)


def last_kernel(n, n_bases, start, near, *refs):
    pieces, w3, bases = refs[:n], refs[n], refs[n + 1 : n + 1 + n_bases]
    out, x, held_out, out_sems = refs[-4:] if near else refs[-6:-2]
    part_steps = bases[0].shape[0] // STEP_ROWS
    steps = part_steps * n_bases

    def copy_out(step, slot):
        rows = pl.ds(start + step * STEP_ROWS, STEP_ROWS)
        return pltpu.make_async_copy(held_out.at[slot], out.at[rows], out_sems.at[slot])

    def body(part, own, step, held):
        slot = lax.rem(step, 2)

        @pl.when(step >= 2)
        def _():
            copy_out(step - 2, slot).wait()

        for t in range(STEP_ROWS):
            y = bases[part][own * STEP_ROWS + t] + mix_rows(held, w3, x.at[t], t)
            split = y.shape[1] // 128
            for h in range(split):
                lines = pl.ds(h, y.shape[0], stride=split)
                held_out[slot, t, lines, :] = y[:, h * 128 : (h + 1) * 128]
        copy_out(step, slot).start()

    if near:
        in_place(pieces, n_bases, part_steps, body)
    else:
        in_steps(pieces, *refs[-2:], n_bases, part_steps, body)
    for step in range(max(steps - 2, 0), steps):
        copy_out(step, step % 2).wait()


def placed(pieces, space):
    return [pltpu.with_memory_space_constraint(piece, space) for piece in pieces]


def held_rows(pieces):
    n, (_, _, chunk, width) = len(pieces), pieces[0].shape
    return pltpu.VMEM((STEP_ROWS, 2 * n * chunk, width), jnp.bfloat16)


def copied_rows(pieces):
    n, (_, _, chunk, width) = len(pieces), pieces[0].shape
    return [
        pltpu.VMEM((2, n, 2, STEP_ROWS, chunk, width), jnp.bfloat16),
        pltpu.SemaphoreType.DMA((2, n)),
    ]


def partial_b(pieces, w3):
    _, local_a, _, width = pieces[0].shape
    n, count = len(pieces), local_a // SUM_ROWS
    vmem = pl.BlockSpec(memory_space=pltpu.VMEM)
    return pl.pallas_call(
        functools.partial(partial_kernel, n),
        in_specs=[pl.BlockSpec(memory_space=pl.ANY)] * n + [vmem],
        out_specs=[vmem] * count,
        out_shape=[pltpu.VMEM((SUM_ROWS, w3.shape[0], width), jnp.float32)] * count,
        scratch_shapes=[held_rows(pieces)] + copied_rows(pieces),
        compiler_params=pltpu.CompilerParams(vmem_limit_bytes=12 << 20),
        name="partial",
    )(*placed(pieces, pltpu.HBM), w3)


def last_b(pieces, w3, bases, out, start, rows, near):
    width = pieces[0].shape[3]
    n, lines = len(pieces), w3.shape[0] * (width // 128)
    vmem = pl.BlockSpec(memory_space=pltpu.VMEM)
    any_space = pl.BlockSpec(memory_space=pl.ANY)
    given = [] if out is None else [out]
    return pl.pallas_call(
        functools.partial(last_kernel, n, len(bases), start, near),
        in_specs=[vmem if near else any_space] * n
        + [vmem] * (1 + len(bases))
        + [any_space] * len(given),
        out_specs=any_space,
        out_shape=jax.ShapeDtypeStruct((rows, lines, 128), jnp.float32),
        input_output_aliases={n + 1 + len(bases): 0} if given else {},
        scratch_shapes=[
            held_rows(pieces),
            pltpu.VMEM((2, STEP_ROWS, lines, 128), jnp.float32),
            pltpu.SemaphoreType.DMA((2,)),
        ]
        + ([] if near else copied_rows(pieces)),
        compiler_params=pltpu.CompilerParams(vmem_limit_bytes=12 << 20),
        name="last",
    )(
        *placed(pieces, pltpu.VMEM if near else pltpu.HBM),
        w3,
        *placed(bases, pltpu.VMEM),
        *given,
    )


def on_device(stem_tensor, branch_one, branch_two, mode_order, branch_three, closing):
    group = lax.axis_size("inter")
    me = lax.axis_index("inter")
    local_a, width = stem_tensor.shape[1], stem_tensor.shape[4]
    size_b = branch_three.shape[1]
    local_b = size_b // group
    chunk = local_b // B_CHUNKS
    size_a = group * local_a
    if (
        local_b % (B_CHUNKS * 2 * ROWS)
        or local_a % ROWS
        or local_a % SUM_ROWS
        or local_a <= LAST_ROWS
        or width % 128
        or stem_tensor.shape[3] != 1
    ):
        return small_blocks(stem_tensor, branch_one, branch_two, mode_order, branch_three, closing)

    rounds = rounds_of(group)
    n_rounds = len(rounds)
    place = me.astype(jnp.uint32)
    zero = jnp.uint32(0)
    target = partners(place, rounds, group)
    pairs = [pairs_of(move, turn, group) for move, turn in rounds]

    def send(block, k):
        if k == 0:
            return block
        return lax.ppermute(block, "inter", pairs[k])

    first = stem_tensor[:, :, :, 0, :]
    stem = lax.optimization_barrier(first)
    arrived = []
    for j in range(B_CHUNKS):
        got = []
        for k in range(n_rounds):
            ahead = j == 0 and k == 1
            block = lax.dynamic_slice(
                first if ahead else stem,
                (zero, zero, target[k] * jnp.uint32(local_b) + jnp.uint32(j * chunk), zero),
                (2, local_a, chunk, width),
                allow_negative_indices=False,
            )
            block = jnp.transpose(block, (0, 2, 1, 3))
            got.append(send(block, k))
        arrived.append(got)
        stem, _ = lax.optimization_barrier((stem, block))

    where_to = jnp.stack(target).astype(jnp.int32)
    where_from = jnp.stack(partners(place, inverse_of(rounds, group), group)).astype(jnp.int32)
    one = branch_one.reshape(2, group, local_a, group, local_a)
    one = one[:, where_from][:, :, :, where_to].reshape(2, size_a, size_a)
    one = jnp.transpose(one, (0, 2, 1))
    w1 = jnp.concatenate(
        [
            jnp.concatenate([one[0], -one[1]], axis=1),
            jnp.concatenate([one[1], one[0]], axis=1),
        ],
        axis=0,
    )
    permuted = jnp.zeros_like(branch_two).at[:, mode_order, :].set(branch_two)
    w2 = jnp.concatenate(
        [
            jnp.concatenate([permuted[0], permuted[1]], axis=1),
            jnp.concatenate([-permuted[1], permuted[0]], axis=1),
        ],
        axis=0,
    )
    close = lax.dynamic_slice_in_dim(closing, me * local_b, local_b, 2).astype(jnp.float32)
    close = close.reshape(2, group, local_a, local_b)[:, where_to].reshape(2, size_a, local_b)
    three = branch_three.reshape(2, group, B_CHUNKS, chunk, size_b)[:, where_from]
    three = jnp.transpose(three, (2, 0, 4, 1, 3)).reshape(B_CHUNKS, 2, size_b, group * chunk)
    w3 = [
        jnp.stack(
            [
                jnp.concatenate([part[0], -part[1]], axis=1),
                jnp.concatenate([part[1], part[0]], axis=1),
            ],
            axis=1,
        ).reshape(2 * size_b, 2 * group * chunk)
        for part in three
    ]
    w1, w2, w3 = lax.optimization_barrier((w1, w2, w3))

    returned = []
    parts = (local_a - LAST_ROWS, LAST_ROWS)
    for j in range(B_CHUNKS):
        splits = parts if j else (local_a,)
        pieces = front(arrived[j], w1, w2, close[:, :, j * chunk : (j + 1) * chunk], splits)
        for i in range(len(splits)):
            returned.append([send(piece, k) for k, piece in enumerate(pieces[i :: len(splits)])])

    sums = partial_b(returned[0], w3[0])
    out, start = None, 0
    for i, count in enumerate(parts):
        own = sums[start // SUM_ROWS : (start + count) // SUM_ROWS]
        out = last_b(returned[1 + i], w3[1], own, out, start, local_a, i == len(parts) - 1)
        start += count
    return out.reshape(local_a, size_b, 2, 1, width)


def solution(mesh):
    in_specs = (P(None, ("cuts", "inter"), None, None, None), P(), P(), P(), P(), P())
    out_specs = P(("cuts", "inter"), None, None, None, None)
    return jax.shard_map(
        on_device, mesh=mesh, in_specs=in_specs, out_specs=out_specs, check_vma=False
    )
```

```python
import functools

import jax
import jax.numpy as jnp
import numpy as np
from jax import lax
from jax.experimental import pallas as pl
from jax.experimental.pallas import tpu as pltpu
from jax.sharding import PartitionSpec as P


B_CHUNKS = 2

ROWS = 8
STEP_ROWS = 2
SUM_ROWS = 8
LAST_ROWS = 8


def complex_mix(input_real, input_imag, weight_real, weight_imag, pattern):

    def product(first_op, second_op):
        return jnp.einsum(pattern, first_op, second_op, preferred_element_type=jnp.float32)

    return (
        product(input_real, weight_real) - product(input_imag, weight_imag),
        product(input_real, weight_imag) + product(input_imag, weight_real),
    )


def small_blocks(stem_tensor, branch_one, branch_two, mode_order, branch_three, closing):
    group_size = lax.axis_size("inter")
    my_index = lax.axis_index("inter")
    local_b = branch_three.shape[1] // group_size
    permuted = jnp.zeros_like(branch_two).at[:, mode_order, :].set(branch_two)
    close_cols = lax.dynamic_slice_in_dim(closing, my_index * local_b, local_b, 2).astype(
        jnp.float32
    )
    close_real = close_cols[0][:, :, None, None]
    close_imag = close_cols[1][:, :, None, None]
    received = lax.all_to_all(stem_tensor, "inter", split_axis=2, concat_axis=1, tiled=True)
    real_part, imag_part = complex_mix(
        received[0], received[1], branch_one[0], branch_one[1], "abkr,ac->cbkr"
    )
    phased = jnp.stack(
        [
            close_real * real_part - close_imag * imag_part,
            close_real * imag_part + close_imag * real_part,
        ]
    ).astype(jnp.bfloat16)
    real_two, imag_two = complex_mix(
        phased[0], phased[1], permuted[0], permuted[1], "abkr,rq->abkq"
    )
    second = jnp.stack([real_two, imag_two]).astype(jnp.bfloat16)
    returned = lax.all_to_all(second, "inter", split_axis=1, concat_axis=2, tiled=True)
    out_real, out_imag = complex_mix(
        returned[0], returned[1], branch_three[0], branch_three[1], "abkr,bc->ackr"
    )
    return jnp.stack([out_real, out_imag], axis=2)


MOVES = ((3, 2, 1, 0), (2, 0, 3, 1), (1, 3, 0, 2))


def rounds_of(group):
    quarters = 4 if group % 4 == 0 else 1
    turns = range(group // quarters)
    moves = MOVES if quarters == 4 else ()
    stay = tuple(range(quarters))
    near = [(stay, t) for t in turns]
    far = [(move, t) for move in moves for t in turns]
    return near[:1] + far[:1] + near[1:] + far[1:]


def inverse_of(rounds, group):
    return [
        (tuple(int(q) for q in np.argsort(move)), -turn % (group // len(move)))
        for move, turn in rounds
    ]


def pairs_of(move, turn, group):
    inner = group // len(move)
    return [
        (i, move[i // inner] * inner + (i % inner + turn) % inner) for i in range(group)
    ]


def partners(index, rounds, group):
    inner = group // len(rounds[0][0])
    quarter, place = index // inner, index % inner
    moved, turned = {}, {}
    for move, turn in rounds:
        if move not in moved:
            steps = [
                jnp.where(quarter == q, jnp.uint32(m * inner), jnp.uint32(0))
                for q, m in enumerate(move)
                if m
            ]
            moved[move] = functools.reduce(jnp.add, steps) if steps else jnp.uint32(0)
        if turn not in turned:
            turned[turn] = (place + jnp.uint32(turn)) % inner
    return [moved[move] + turned[turn] for move, turn in rounds]


def first_block_kernel(index, piece, out, turned):
    _, rows, chunk, width = piece.shape
    for c in range(2):
        for h in range(width // 128):
            lanes = slice(h * 128, (h + 1) * 128)
            for a in range(rows):
                turned[c, h, pl.ds(a, chunk, stride=rows), :] = piece[c, a, :, lanes].astype(
                    jnp.float32
                )
            out[c, :, :, lanes] = (
                turned[c, h].reshape(chunk, rows, 128).astype(jnp.bfloat16)
            )


def first_block(stem, index, chunk):
    _, local_a, _, width = stem.shape
    return pl.pallas_call(
        first_block_kernel,
        grid_spec=pltpu.PrefetchScalarGridSpec(
            num_scalar_prefetch=1,
            grid=(local_a // ROWS,),
            in_specs=[pl.BlockSpec((2, ROWS, chunk, width), lambda a, index: (0, a, index[0], 0))],
            out_specs=pl.BlockSpec((2, chunk, ROWS, width), lambda a, index: (0, 0, a, 0)),
            scratch_shapes=[pltpu.VMEM((2, width // 128, chunk * ROWS, 128), jnp.float32)],
        ),
        out_shape=pltpu.HBM((2, chunk, local_a, width), jnp.bfloat16),
        compiler_params=pltpu.CompilerParams(vmem_limit_bytes=4 << 20),
        name="first_block",
    )(index.astype(jnp.int32).reshape(1), stem)


def front_kernel(group, splits, *refs):
    pieces, (w1, w2, close), outs = refs[:group], refs[group : group + 3], refs[group + 3 : -2]
    x, acc = refs[-2:]
    step = pl.program_id(0)
    local_a, width = pieces[0].shape[2:]
    total = group * local_a
    for i, piece in enumerate(pieces):
        for c in range(2):
            x[c * total + i * local_a : c * total + (i + 1) * local_a, :] = piece[c, 0]
    y = jnp.dot(w1[...], x[...], preferred_element_type=jnp.float32)
    lane = lax.broadcasted_iota(jnp.int32, close.shape[1:], 1)

    def column(c):
        return jnp.sum(jnp.where(lane == step, close[c], 0.0), axis=1, keepdims=True)

    cr, ci = column(0), column(1)
    yr, yi = y[:total], y[total:]
    phased = jnp.concatenate(
        [(cr * yr - ci * yi).astype(jnp.bfloat16), (cr * yi + ci * yr).astype(jnp.bfloat16)],
        axis=1,
    )
    both = jnp.dot(phased, w2[...], preferred_element_type=jnp.float32)
    row = lax.rem(step, ROWS)
    for h in range(acc.shape[0]):
        acc[h, pl.ds(row, total, stride=ROWS), :] = both[:, h * 128 : (h + 1) * 128]

    @pl.when(row == ROWS - 1)
    def _():
        first = 0
        for i, out in enumerate(outs):
            count = splits[i % len(splits)]
            for h in range(acc.shape[0]):
                c, lanes = divmod(h * 128, width)
                out[c, :, :, lanes : lanes + 128] = (
                    acc[h, first * ROWS : (first + count) * ROWS, :]
                    .reshape(count, ROWS, 128)
                    .astype(jnp.bfloat16)
                )
            first += count


def front(pieces, w1, w2, close, splits):
    group = len(pieces)
    _, chunk, local_a, width = pieces[0].shape
    total = group * local_a
    return pl.pallas_call(
        functools.partial(front_kernel, group, splits),
        grid=(chunk,),
        in_specs=[pl.BlockSpec((2, 1, local_a, width), lambda b: (0, b, 0, 0))] * group
        + [
            pl.BlockSpec(w1.shape, lambda b: (0, 0)),
            pl.BlockSpec(w2.shape, lambda b: (0, 0)),
            pl.BlockSpec(close.shape, lambda b: (0, 0, 0)),
        ],
        out_specs=[
            pl.BlockSpec((2, count, ROWS, width), lambda b: (0, 0, b // ROWS, 0))
            for count in splits
        ]
        * group,
        out_shape=[pltpu.HBM((2, count, chunk, width), jnp.bfloat16) for count in splits] * group,
        scratch_shapes=[
            pltpu.VMEM((2 * total, width), jnp.bfloat16),
            pltpu.VMEM((2 * width // 128, total * ROWS, 128), jnp.float32),
        ],
        compiler_params=pltpu.CompilerParams(vmem_limit_bytes=40 << 20),
        name="front",
    )(*pieces, w1, w2, close)


def mix_rows(pieces, w3, x, t):
    chunk, _ = pieces[0].shape[2:]
    total = len(pieces) * chunk
    for i, piece in enumerate(pieces):
        for c in range(2):
            x[c * total + i * chunk : c * total + (i + 1) * chunk, :] = piece[c, t]
    return jnp.dot(w3[...], x[...], preferred_element_type=jnp.float32)


def in_place(pieces, parts, steps, body):
    for part in range(parts):

        @pl.loop(0, steps)
        def _(own):
            step = part * steps + own
            rows = pl.ds(step * STEP_ROWS, STEP_ROWS)
            body(part, own, step, [piece.at[:, rows] for piece in pieces])


def in_steps(pieces, buffers, sems, parts, steps, body):
    def copies(step, slot):
        rows = pl.ds(step * STEP_ROWS, STEP_ROWS)
        return [
            pltpu.make_async_copy(piece.at[:, rows], buffers.at[slot, i], sems.at[slot, i])
            for i, piece in enumerate(pieces)
        ]

    for copy in copies(0, 0):
        copy.start()
    for part in range(parts):

        @pl.loop(0, steps)
        def _(own):
            step = part * steps + own
            slot = lax.rem(step, 2)

            @pl.when(step + 1 < parts * steps)
            def _():
                for copy in copies(step + 1, 1 - slot):
                    copy.start()

            for copy in copies(step, slot):
                copy.wait()
            body(part, own, step, [buffers.at[slot, i] for i in range(len(pieces))])


def partial_kernel(n, *refs):
    pieces, w3, outs, (x, buffers, sems) = refs[:n], refs[n], refs[n + 1 : -3], refs[-3:]

    def body(part, own, step, held):
        for t in range(STEP_ROWS):
            outs[part][own * STEP_ROWS + t] = mix_rows(held, w3, x.at[t], t)

    in_steps(pieces, buffers, sems, len(outs), outs[0].shape[0] // STEP_ROWS, body)


def last_kernel(n, n_bases, start, near, *refs):
    pieces, w3, bases = refs[:n], refs[n], refs[n + 1 : n + 1 + n_bases]
    out, x, held_out, out_sems = refs[-4:] if near else refs[-6:-2]
    part_steps = bases[0].shape[0] // STEP_ROWS
    steps = part_steps * n_bases

    def copy_out(step, slot):
        rows = pl.ds(start + step * STEP_ROWS, STEP_ROWS)
        return pltpu.make_async_copy(held_out.at[slot], out.at[rows], out_sems.at[slot])

    def body(part, own, step, held):
        slot = lax.rem(step, 2)

        @pl.when(step >= 2)
        def _():
            copy_out(step - 2, slot).wait()

        for t in range(STEP_ROWS):
            y = bases[part][own * STEP_ROWS + t] + mix_rows(held, w3, x.at[t], t)
            split = y.shape[1] // 128
            for h in range(split):
                lines = pl.ds(h, y.shape[0], stride=split)
                held_out[slot, t, lines, :] = y[:, h * 128 : (h + 1) * 128]
        copy_out(step, slot).start()

    if near:
        in_place(pieces, n_bases, part_steps, body)
    else:
        in_steps(pieces, *refs[-2:], n_bases, part_steps, body)
    for step in range(max(steps - 2, 0), steps):
        copy_out(step, step % 2).wait()


def placed(pieces, space):
    return [pltpu.with_memory_space_constraint(piece, space) for piece in pieces]


def held_rows(pieces):
    n, (_, _, chunk, width) = len(pieces), pieces[0].shape
    return pltpu.VMEM((STEP_ROWS, 2 * n * chunk, width), jnp.bfloat16)


def copied_rows(pieces):
    n, (_, _, chunk, width) = len(pieces), pieces[0].shape
    return [
        pltpu.VMEM((2, n, 2, STEP_ROWS, chunk, width), jnp.bfloat16),
        pltpu.SemaphoreType.DMA((2, n)),
    ]


def partial_b(pieces, w3):
    _, local_a, _, width = pieces[0].shape
    n, count = len(pieces), local_a // SUM_ROWS
    vmem = pl.BlockSpec(memory_space=pltpu.VMEM)
    return pl.pallas_call(
        functools.partial(partial_kernel, n),
        in_specs=[pl.BlockSpec(memory_space=pl.ANY)] * n + [vmem],
        out_specs=[vmem] * count,
        out_shape=[pltpu.VMEM((SUM_ROWS, w3.shape[0], width), jnp.float32)] * count,
        scratch_shapes=[held_rows(pieces)] + copied_rows(pieces),
        compiler_params=pltpu.CompilerParams(vmem_limit_bytes=12 << 20),
        name="partial",
    )(*placed(pieces, pltpu.HBM), w3)


def last_b(pieces, w3, bases, out, start, rows, near):
    width = pieces[0].shape[3]
    n, lines = len(pieces), w3.shape[0] * (width // 128)
    vmem = pl.BlockSpec(memory_space=pltpu.VMEM)
    any_space = pl.BlockSpec(memory_space=pl.ANY)
    given = [] if out is None else [out]
    return pl.pallas_call(
        functools.partial(last_kernel, n, len(bases), start, near),
        in_specs=[vmem if near else any_space] * n
        + [vmem] * (1 + len(bases))
        + [any_space] * len(given),
        out_specs=any_space,
        out_shape=jax.ShapeDtypeStruct((rows, lines, 128), jnp.float32),
        input_output_aliases={n + 1 + len(bases): 0} if given else {},
        scratch_shapes=[
            held_rows(pieces),
            pltpu.VMEM((2, STEP_ROWS, lines, 128), jnp.float32),
            pltpu.SemaphoreType.DMA((2,)),
        ]
        + ([] if near else copied_rows(pieces)),
        compiler_params=pltpu.CompilerParams(vmem_limit_bytes=12 << 20),
        name="last",
    )(
        *placed(pieces, pltpu.VMEM if near else pltpu.HBM),
        w3,
        *placed(bases, pltpu.VMEM),
        *given,
    )


def on_device(stem_tensor, branch_one, branch_two, mode_order, branch_three, closing):
    group = lax.axis_size("inter")
    me = lax.axis_index("inter")
    local_a, width = stem_tensor.shape[1], stem_tensor.shape[4]
    size_b = branch_three.shape[1]
    local_b = size_b // group
    chunk = local_b // B_CHUNKS
    size_a = group * local_a
    if (
        local_b % (B_CHUNKS * 2 * ROWS)
        or local_a % ROWS
        or local_a % SUM_ROWS
        or local_a <= LAST_ROWS
        or width % 128
        or stem_tensor.shape[3] != 1
    ):
        return small_blocks(stem_tensor, branch_one, branch_two, mode_order, branch_three, closing)

    rounds = rounds_of(group)
    n_rounds = len(rounds)
    place = me.astype(jnp.uint32)
    zero = jnp.uint32(0)
    target = partners(place, rounds, group)
    pairs = [pairs_of(move, turn, group) for move, turn in rounds]

    def send(block, k):
        if k == 0:
            return block
        return lax.ppermute(block, "inter", pairs[k])

    stem = stem_tensor[:, :, :, 0, :]
    arrived = []
    for j in range(B_CHUNKS):
        got = []
        for k in range(n_rounds):
            start = target[k] * jnp.uint32(B_CHUNKS) + jnp.uint32(j)
            ahead = j == 0 and k == 1
            if ahead:
                block = first_block(stem, start, chunk)
            else:
                block = lax.dynamic_slice(
                    stem,
                    (zero, zero, start * jnp.uint32(chunk), zero),
                    (2, local_a, chunk, width),
                    allow_negative_indices=False,
                )
                block = jnp.transpose(block, (0, 2, 1, 3))
            got.append(send(block, k))
        arrived.append(got)

    where_to = jnp.stack(target).astype(jnp.int32)
    where_from = jnp.stack(partners(place, inverse_of(rounds, group), group)).astype(jnp.int32)
    one = branch_one.reshape(2, group, local_a, group, local_a)
    one = one[:, where_from][:, :, :, where_to].reshape(2, size_a, size_a)
    one = jnp.transpose(one, (0, 2, 1))
    w1 = jnp.concatenate(
        [
            jnp.concatenate([one[0], -one[1]], axis=1),
            jnp.concatenate([one[1], one[0]], axis=1),
        ],
        axis=0,
    )
    permuted = jnp.zeros_like(branch_two).at[:, mode_order, :].set(branch_two)
    w2 = jnp.concatenate(
        [
            jnp.concatenate([permuted[0], permuted[1]], axis=1),
            jnp.concatenate([-permuted[1], permuted[0]], axis=1),
        ],
        axis=0,
    )
    close = lax.dynamic_slice_in_dim(closing, me * local_b, local_b, 2).astype(jnp.float32)
    close = close.reshape(2, group, local_a, local_b)[:, where_to].reshape(2, size_a, local_b)
    three = branch_three.reshape(2, group, B_CHUNKS, chunk, size_b)[:, where_from]
    three = jnp.transpose(three, (2, 0, 4, 1, 3)).reshape(B_CHUNKS, 2, size_b, group * chunk)
    w3 = [
        jnp.stack(
            [
                jnp.concatenate([part[0], -part[1]], axis=1),
                jnp.concatenate([part[1], part[0]], axis=1),
            ],
            axis=1,
        ).reshape(2 * size_b, 2 * group * chunk)
        for part in three
    ]
    w1, w2, w3 = lax.optimization_barrier((w1, w2, w3))

    returned = []
    parts = (local_a - LAST_ROWS, LAST_ROWS)
    for j in range(B_CHUNKS):
        splits = parts if j else (local_a,)
        pieces = front(arrived[j], w1, w2, close[:, :, j * chunk : (j + 1) * chunk], splits)
        for i in range(len(splits)):
            returned.append([send(piece, k) for k, piece in enumerate(pieces[i :: len(splits)])])

    sums = partial_b(returned[0], w3[0])
    out, start = None, 0
    for i, count in enumerate(parts):
        own = sums[start // SUM_ROWS : (start + count) // SUM_ROWS]
        out = last_b(returned[1 + i], w3[1], own, out, start, local_a, i == len(parts) - 1)
        start += count
    return out.reshape(local_a, size_b, 2, 1, width)


def solution(mesh):
    in_specs = (P(None, ("cuts", "inter"), None, None, None), P(), P(), P(), P(), P())
    out_specs = P(("cuts", "inter"), None, None, None, None)
    return jax.shard_map(
        on_device, mesh=mesh, in_specs=in_specs, out_specs=out_specs, check_vma=False
    )
```

```python
import functools

import jax
import jax.numpy as jnp
import numpy as np
from jax import lax
from jax.experimental import pallas as pl
from jax.experimental.pallas import tpu as pltpu
from jax.sharding import PartitionSpec as P


B_CHUNKS = 2

ROWS = 8
STEP_ROWS = 2
SUM_ROWS = 8
LAST_ROWS = 8


def complex_mix(input_real, input_imag, weight_real, weight_imag, pattern):

    def product(first_op, second_op):
        return jnp.einsum(pattern, first_op, second_op, preferred_element_type=jnp.float32)

    return (
        product(input_real, weight_real) - product(input_imag, weight_imag),
        product(input_real, weight_imag) + product(input_imag, weight_real),
    )


def small_blocks(stem_tensor, branch_one, branch_two, mode_order, branch_three, closing):
    group_size = lax.axis_size("inter")
    my_index = lax.axis_index("inter")
    local_b = branch_three.shape[1] // group_size
    permuted = jnp.zeros_like(branch_two).at[:, mode_order, :].set(branch_two)
    close_cols = lax.dynamic_slice_in_dim(closing, my_index * local_b, local_b, 2).astype(
        jnp.float32
    )
    close_real = close_cols[0][:, :, None, None]
    close_imag = close_cols[1][:, :, None, None]
    received = lax.all_to_all(stem_tensor, "inter", split_axis=2, concat_axis=1, tiled=True)
    real_part, imag_part = complex_mix(
        received[0], received[1], branch_one[0], branch_one[1], "abkr,ac->cbkr"
    )
    phased = jnp.stack(
        [
            close_real * real_part - close_imag * imag_part,
            close_real * imag_part + close_imag * real_part,
        ]
    ).astype(jnp.bfloat16)
    real_two, imag_two = complex_mix(
        phased[0], phased[1], permuted[0], permuted[1], "abkr,rq->abkq"
    )
    second = jnp.stack([real_two, imag_two]).astype(jnp.bfloat16)
    returned = lax.all_to_all(second, "inter", split_axis=1, concat_axis=2, tiled=True)
    out_real, out_imag = complex_mix(
        returned[0], returned[1], branch_three[0], branch_three[1], "abkr,bc->ackr"
    )
    return jnp.stack([out_real, out_imag], axis=2)


MOVES = ((3, 2, 1, 0), (2, 0, 3, 1), (1, 3, 0, 2))


def rounds_of(group):
    quarters = 4 if group % 4 == 0 else 1
    turns = range(group // quarters)
    moves = MOVES if quarters == 4 else ()
    stay = tuple(range(quarters))
    near = [(stay, t) for t in turns]
    far = [(move, t) for move in moves for t in turns]
    return near[:1] + far[:1] + near[1:] + far[1:]


def inverse_of(rounds, group):
    return [
        (tuple(int(q) for q in np.argsort(move)), -turn % (group // len(move)))
        for move, turn in rounds
    ]


def pairs_of(move, turn, group):
    inner = group // len(move)
    return [
        (i, move[i // inner] * inner + (i % inner + turn) % inner) for i in range(group)
    ]


def partners(index, rounds, group):
    inner = group // len(rounds[0][0])
    quarter, place = index // inner, index % inner
    kind = jnp.uint32 if index.dtype == jnp.uint32 else jnp.int32
    moved, turned = {}, {}
    for move, turn in rounds:
        if move not in moved:
            steps = [
                jnp.where(quarter == q, kind(m * inner), kind(0)) for q, m in enumerate(move) if m
            ]
            moved[move] = functools.reduce(jnp.add, steps) if steps else kind(0)
        if turn not in turned:
            turned[turn] = (place + kind(turn)) % inner
    return [moved[move] + turned[turn] for move, turn in rounds]


def first_block_kernel(move_turn, group, stem, out, held, turned, sems):
    local_a, width = stem.shape[1], stem.shape[3]
    chunk = out.shape[1]
    (target,) = partners(lax.axis_index("inter"), [move_turn], group)
    columns = pl.ds(pl.multiple_of(target * (stem.shape[2] // group), chunk), chunk)
    copies = []
    for i in range(local_a // ROWS):
        rows = slice(i * ROWS, (i + 1) * ROWS)
        copies.append(
            pltpu.make_async_copy(stem.at[:, rows, columns], held.at[:, rows], sems.at[i])
        )
        copies[-1].start()
    for i, copy in enumerate(copies):
        copy.wait()
        for c in range(2):
            for h in range(width // 128):
                lanes = slice(h * 128, (h + 1) * 128)
                for a in range(ROWS):
                    turned[c, h, pl.ds(a, chunk, stride=ROWS), :] = held[
                        c, i * ROWS + a, :, lanes
                    ].astype(jnp.float32)
                out[c, :, i * ROWS : (i + 1) * ROWS, lanes] = (
                    turned[c, h].reshape(chunk, ROWS, 128).astype(jnp.bfloat16)
                )


def first_block(stem, move_turn, group, chunk):
    _, local_a, _, width = stem.shape
    return pl.pallas_call(
        functools.partial(first_block_kernel, move_turn, group),
        in_specs=[pl.BlockSpec(memory_space=pl.ANY)],
        out_specs=pl.BlockSpec(memory_space=pltpu.VMEM),
        out_shape=pltpu.VMEM((2, chunk, local_a, width), jnp.bfloat16),
        scratch_shapes=[
            pltpu.VMEM((2, local_a, chunk, width), jnp.bfloat16),
            pltpu.VMEM((2, width // 128, chunk * ROWS, 128), jnp.float32),
            pltpu.SemaphoreType.DMA((local_a // ROWS,)),
        ],
        compiler_params=pltpu.CompilerParams(vmem_limit_bytes=4 << 20),
        name="first_block",
    )(*placed([stem], pltpu.HBM))


def front_kernel(group, splits, *refs):
    pieces, (w1, w2, close), outs = refs[:group], refs[group : group + 3], refs[group + 3 : -2]
    x, acc = refs[-2:]
    step = pl.program_id(0)
    local_a, width = pieces[0].shape[2:]
    total = group * local_a
    for i, piece in enumerate(pieces):
        for c in range(2):
            x[c * total + i * local_a : c * total + (i + 1) * local_a, :] = piece[c, 0]
    y = jnp.dot(w1[...], x[...], preferred_element_type=jnp.float32)
    lane = lax.broadcasted_iota(jnp.int32, close.shape[1:], 1)

    def column(c):
        return jnp.sum(jnp.where(lane == step, close[c], 0.0), axis=1, keepdims=True)

    cr, ci = column(0), column(1)
    yr, yi = y[:total], y[total:]
    phased = jnp.concatenate(
        [(cr * yr - ci * yi).astype(jnp.bfloat16), (cr * yi + ci * yr).astype(jnp.bfloat16)],
        axis=1,
    )
    both = jnp.dot(phased, w2[...], preferred_element_type=jnp.float32)
    row = lax.rem(step, ROWS)
    for h in range(acc.shape[0]):
        acc[h, pl.ds(row, total, stride=ROWS), :] = both[:, h * 128 : (h + 1) * 128]

    @pl.when(row == ROWS - 1)
    def _():
        first = 0
        for i, out in enumerate(outs):
            count = splits[i % len(splits)]
            for h in range(acc.shape[0]):
                c, lanes = divmod(h * 128, width)
                out[c, :, :, lanes : lanes + 128] = (
                    acc[h, first * ROWS : (first + count) * ROWS, :]
                    .reshape(count, ROWS, 128)
                    .astype(jnp.bfloat16)
                )
            first += count


def front(pieces, w1, w2, close, splits):
    group = len(pieces)
    _, chunk, local_a, width = pieces[0].shape
    total = group * local_a
    return pl.pallas_call(
        functools.partial(front_kernel, group, splits),
        grid=(chunk,),
        in_specs=[pl.BlockSpec((2, 1, local_a, width), lambda b: (0, b, 0, 0))] * group
        + [
            pl.BlockSpec(w1.shape, lambda b: (0, 0)),
            pl.BlockSpec(w2.shape, lambda b: (0, 0)),
            pl.BlockSpec(close.shape, lambda b: (0, 0, 0)),
        ],
        out_specs=[
            pl.BlockSpec((2, count, ROWS, width), lambda b: (0, 0, b // ROWS, 0))
            for count in splits
        ]
        * group,
        out_shape=[pltpu.HBM((2, count, chunk, width), jnp.bfloat16) for count in splits] * group,
        scratch_shapes=[
            pltpu.VMEM((2 * total, width), jnp.bfloat16),
            pltpu.VMEM((2 * width // 128, total * ROWS, 128), jnp.float32),
        ],
        compiler_params=pltpu.CompilerParams(vmem_limit_bytes=40 << 20),
        name="front",
    )(*pieces, w1, w2, close)


def mix_rows(pieces, w3, x, t):
    chunk, _ = pieces[0].shape[2:]
    total = len(pieces) * chunk
    for i, piece in enumerate(pieces):
        for c in range(2):
            x[c * total + i * chunk : c * total + (i + 1) * chunk, :] = piece[c, t]
    return jnp.dot(w3[...], x[...], preferred_element_type=jnp.float32)


def in_place(pieces, parts, steps, body):
    for part in range(parts):

        @pl.loop(0, steps)
        def _(own):
            step = part * steps + own
            rows = pl.ds(step * STEP_ROWS, STEP_ROWS)
            body(part, own, step, [piece.at[:, rows] for piece in pieces])


def in_steps(pieces, buffers, sems, parts, steps, body):
    def copies(step, slot):
        rows = pl.ds(step * STEP_ROWS, STEP_ROWS)
        return [
            pltpu.make_async_copy(piece.at[:, rows], buffers.at[slot, i], sems.at[slot, i])
            for i, piece in enumerate(pieces)
        ]

    for copy in copies(0, 0):
        copy.start()
    for part in range(parts):

        @pl.loop(0, steps)
        def _(own):
            step = part * steps + own
            slot = lax.rem(step, 2)

            @pl.when(step + 1 < parts * steps)
            def _():
                for copy in copies(step + 1, 1 - slot):
                    copy.start()

            for copy in copies(step, slot):
                copy.wait()
            body(part, own, step, [buffers.at[slot, i] for i in range(len(pieces))])


def partial_kernel(n, *refs):
    pieces, w3, outs, (x, buffers, sems) = refs[:n], refs[n], refs[n + 1 : -3], refs[-3:]

    def body(part, own, step, held):
        for t in range(STEP_ROWS):
            outs[part][own * STEP_ROWS + t] = mix_rows(held, w3, x.at[t], t)

    in_steps(pieces, buffers, sems, len(outs), outs[0].shape[0] // STEP_ROWS, body)


def last_kernel(n, n_bases, start, near, *refs):
    pieces, w3, bases = refs[:n], refs[n], refs[n + 1 : n + 1 + n_bases]
    out, x, held_out, out_sems = refs[-4:] if near else refs[-6:-2]
    part_steps = bases[0].shape[0] // STEP_ROWS
    steps = part_steps * n_bases

    def copy_out(step, slot):
        rows = pl.ds(start + step * STEP_ROWS, STEP_ROWS)
        return pltpu.make_async_copy(held_out.at[slot], out.at[rows], out_sems.at[slot])

    def body(part, own, step, held):
        slot = lax.rem(step, 2)

        @pl.when(step >= 2)
        def _():
            copy_out(step - 2, slot).wait()

        for t in range(STEP_ROWS):
            y = bases[part][own * STEP_ROWS + t] + mix_rows(held, w3, x.at[t], t)
            split = y.shape[1] // 128
            for h in range(split):
                lines = pl.ds(h, y.shape[0], stride=split)
                held_out[slot, t, lines, :] = y[:, h * 128 : (h + 1) * 128]
        copy_out(step, slot).start()

    if near:
        in_place(pieces, n_bases, part_steps, body)
    else:
        in_steps(pieces, *refs[-2:], n_bases, part_steps, body)
    for step in range(max(steps - 2, 0), steps):
        copy_out(step, step % 2).wait()


def placed(pieces, space):
    return [pltpu.with_memory_space_constraint(piece, space) for piece in pieces]


def held_rows(pieces):
    n, (_, _, chunk, width) = len(pieces), pieces[0].shape
    return pltpu.VMEM((STEP_ROWS, 2 * n * chunk, width), jnp.bfloat16)


def copied_rows(pieces):
    n, (_, _, chunk, width) = len(pieces), pieces[0].shape
    return [
        pltpu.VMEM((2, n, 2, STEP_ROWS, chunk, width), jnp.bfloat16),
        pltpu.SemaphoreType.DMA((2, n)),
    ]


def partial_b(pieces, w3):
    _, local_a, _, width = pieces[0].shape
    n, count = len(pieces), local_a // SUM_ROWS
    vmem = pl.BlockSpec(memory_space=pltpu.VMEM)
    return pl.pallas_call(
        functools.partial(partial_kernel, n),
        in_specs=[pl.BlockSpec(memory_space=pl.ANY)] * n + [vmem],
        out_specs=[vmem] * count,
        out_shape=[pltpu.VMEM((SUM_ROWS, w3.shape[0], width), jnp.float32)] * count,
        scratch_shapes=[held_rows(pieces)] + copied_rows(pieces),
        compiler_params=pltpu.CompilerParams(vmem_limit_bytes=12 << 20),
        name="partial",
    )(*placed(pieces, pltpu.HBM), w3)


def last_b(pieces, w3, bases, out, start, rows, near):
    width = pieces[0].shape[3]
    n, lines = len(pieces), w3.shape[0] * (width // 128)
    vmem = pl.BlockSpec(memory_space=pltpu.VMEM)
    any_space = pl.BlockSpec(memory_space=pl.ANY)
    given = [] if out is None else [out]
    return pl.pallas_call(
        functools.partial(last_kernel, n, len(bases), start, near),
        in_specs=[vmem if near else any_space] * n
        + [vmem] * (1 + len(bases))
        + [any_space] * len(given),
        out_specs=any_space,
        out_shape=jax.ShapeDtypeStruct((rows, lines, 128), jnp.float32),
        input_output_aliases={n + 1 + len(bases): 0} if given else {},
        scratch_shapes=[
            held_rows(pieces),
            pltpu.VMEM((2, STEP_ROWS, lines, 128), jnp.float32),
            pltpu.SemaphoreType.DMA((2,)),
        ]
        + ([] if near else copied_rows(pieces)),
        compiler_params=pltpu.CompilerParams(vmem_limit_bytes=12 << 20),
        name="last",
    )(
        *placed(pieces, pltpu.VMEM if near else pltpu.HBM),
        w3,
        *placed(bases, pltpu.VMEM),
        *given,
    )


def on_device(stem_tensor, branch_one, branch_two, mode_order, branch_three, closing):
    group = lax.axis_size("inter")
    me = lax.axis_index("inter")
    local_a, width = stem_tensor.shape[1], stem_tensor.shape[4]
    size_b = branch_three.shape[1]
    local_b = size_b // group
    chunk = local_b // B_CHUNKS
    size_a = group * local_a
    if (
        local_b % (B_CHUNKS * 2 * ROWS)
        or local_a % ROWS
        or local_a % SUM_ROWS
        or local_a <= LAST_ROWS
        or width % 128
        or stem_tensor.shape[3] != 1
    ):
        return small_blocks(stem_tensor, branch_one, branch_two, mode_order, branch_three, closing)

    rounds = rounds_of(group)
    n_rounds = len(rounds)
    place = me.astype(jnp.uint32)
    zero = jnp.uint32(0)
    target = partners(place, rounds, group)
    pairs = [pairs_of(move, turn, group) for move, turn in rounds]

    def send(block, k):
        if k == 0:
            return block
        return lax.ppermute(block, "inter", pairs[k])

    stem = stem_tensor[:, :, :, 0, :]
    arrived = []
    for j in range(B_CHUNKS):
        got = []
        for k in range(n_rounds):
            start = target[k] * jnp.uint32(B_CHUNKS) + jnp.uint32(j)
            ahead = j == 0 and k == 1
            if ahead:
                block = first_block(stem, rounds[k], group, chunk)
            else:
                block = lax.dynamic_slice(
                    stem,
                    (zero, zero, start * jnp.uint32(chunk), zero),
                    (2, local_a, chunk, width),
                    allow_negative_indices=False,
                )
                block = jnp.transpose(block, (0, 2, 1, 3))
            got.append(send(block, k))
        arrived.append(got)

    where_to = jnp.stack(target).astype(jnp.int32)
    where_from = jnp.stack(partners(place, inverse_of(rounds, group), group)).astype(jnp.int32)
    one = branch_one.reshape(2, group, local_a, group, local_a)
    one = one[:, where_from][:, :, :, where_to].reshape(2, size_a, size_a)
    one = jnp.transpose(one, (0, 2, 1))
    w1 = jnp.concatenate(
        [
            jnp.concatenate([one[0], -one[1]], axis=1),
            jnp.concatenate([one[1], one[0]], axis=1),
        ],
        axis=0,
    )
    permuted = jnp.zeros_like(branch_two).at[:, mode_order, :].set(branch_two)
    w2 = jnp.concatenate(
        [
            jnp.concatenate([permuted[0], permuted[1]], axis=1),
            jnp.concatenate([-permuted[1], permuted[0]], axis=1),
        ],
        axis=0,
    )
    close = lax.dynamic_slice_in_dim(closing, me * local_b, local_b, 2).astype(jnp.float32)
    close = close.reshape(2, group, local_a, local_b)[:, where_to].reshape(2, size_a, local_b)
    three = branch_three.reshape(2, group, B_CHUNKS, chunk, size_b)[:, where_from]
    three = jnp.transpose(three, (2, 0, 4, 1, 3)).reshape(B_CHUNKS, 2, size_b, group * chunk)
    w3 = [
        jnp.stack(
            [
                jnp.concatenate([part[0], -part[1]], axis=1),
                jnp.concatenate([part[1], part[0]], axis=1),
            ],
            axis=1,
        ).reshape(2 * size_b, 2 * group * chunk)
        for part in three
    ]
    w1, w2, w3 = lax.optimization_barrier((w1, w2, w3))

    returned = []
    parts = (local_a - LAST_ROWS, LAST_ROWS)
    for j in range(B_CHUNKS):
        splits = parts if j else (local_a,)
        pieces = front(arrived[j], w1, w2, close[:, :, j * chunk : (j + 1) * chunk], splits)
        for i in range(len(splits)):
            returned.append([send(piece, k) for k, piece in enumerate(pieces[i :: len(splits)])])

    sums = partial_b(returned[0], w3[0])
    out, start = None, 0
    for i, count in enumerate(parts):
        own = sums[start // SUM_ROWS : (start + count) // SUM_ROWS]
        out = last_b(returned[1 + i], w3[1], own, out, start, local_a, i == len(parts) - 1)
        start += count
    return out.reshape(local_a, size_b, 2, 1, width)


def solution(mesh):
    in_specs = (P(None, ("cuts", "inter"), None, None, None), P(), P(), P(), P(), P())
    out_specs = P(("cuts", "inter"), None, None, None, None)
    return jax.shard_map(
        on_device, mesh=mesh, in_specs=in_specs, out_specs=out_specs, check_vma=False
    )
```

```python
import functools

import jax
import jax.numpy as jnp
import numpy as np
from jax import lax
from jax.experimental import pallas as pl
from jax.experimental.pallas import tpu as pltpu
from jax.sharding import PartitionSpec as P


B_CHUNKS = 2

ROWS = 8
STEP_ROWS = 2
SUM_ROWS = 8
LATE_ROWS = (8, 2)


def complex_mix(input_real, input_imag, weight_real, weight_imag, pattern):

    def product(first_op, second_op):
        return jnp.einsum(pattern, first_op, second_op, preferred_element_type=jnp.float32)

    return (
        product(input_real, weight_real) - product(input_imag, weight_imag),
        product(input_real, weight_imag) + product(input_imag, weight_real),
    )


def small_blocks(stem_tensor, branch_one, branch_two, mode_order, branch_three, closing):
    group_size = lax.axis_size("inter")
    my_index = lax.axis_index("inter")
    local_b = branch_three.shape[1] // group_size
    permuted = jnp.zeros_like(branch_two).at[:, mode_order, :].set(branch_two)
    close_cols = lax.dynamic_slice_in_dim(closing, my_index * local_b, local_b, 2).astype(
        jnp.float32
    )
    close_real = close_cols[0][:, :, None, None]
    close_imag = close_cols[1][:, :, None, None]
    received = lax.all_to_all(stem_tensor, "inter", split_axis=2, concat_axis=1, tiled=True)
    real_part, imag_part = complex_mix(
        received[0], received[1], branch_one[0], branch_one[1], "abkr,ac->cbkr"
    )
    phased = jnp.stack(
        [
            close_real * real_part - close_imag * imag_part,
            close_real * imag_part + close_imag * real_part,
        ]
    ).astype(jnp.bfloat16)
    real_two, imag_two = complex_mix(
        phased[0], phased[1], permuted[0], permuted[1], "abkr,rq->abkq"
    )
    second = jnp.stack([real_two, imag_two]).astype(jnp.bfloat16)
    returned = lax.all_to_all(second, "inter", split_axis=1, concat_axis=2, tiled=True)
    out_real, out_imag = complex_mix(
        returned[0], returned[1], branch_three[0], branch_three[1], "abkr,bc->ackr"
    )
    return jnp.stack([out_real, out_imag], axis=2)


MOVES = ((3, 2, 1, 0), (2, 0, 3, 1), (1, 3, 0, 2))


def rounds_of(group):
    quarters = 4 if group % 4 == 0 else 1
    turns = range(group // quarters)
    moves = MOVES if quarters == 4 else ()
    stay = tuple(range(quarters))
    near = [(stay, t) for t in turns]
    far = [(move, t) for move in moves for t in turns]
    return near[:1] + far[:1] + near[1:] + far[1:]


def inverse_of(rounds, group):
    return [
        (tuple(int(q) for q in np.argsort(move)), -turn % (group // len(move)))
        for move, turn in rounds
    ]


def pairs_of(move, turn, group):
    inner = group // len(move)
    return [
        (i, move[i // inner] * inner + (i % inner + turn) % inner) for i in range(group)
    ]


def partners(index, rounds, group):
    inner = group // len(rounds[0][0])
    quarter, place = index // inner, index % inner
    kind = jnp.uint32 if index.dtype == jnp.uint32 else jnp.int32
    moved, turned = {}, {}
    for move, turn in rounds:
        if move not in moved:
            steps = [
                jnp.where(quarter == q, kind(m * inner), kind(0)) for q, m in enumerate(move) if m
            ]
            moved[move] = functools.reduce(jnp.add, steps) if steps else kind(0)
        if turn not in turned:
            turned[turn] = (place + kind(turn)) % inner
    return [moved[move] + turned[turn] for move, turn in rounds]


def first_block_kernel(move_turn, group, stem, out, held, turned, sems):
    local_a, width = stem.shape[1], stem.shape[3]
    chunk = out.shape[1]
    (target,) = partners(lax.axis_index("inter"), [move_turn], group)
    columns = pl.ds(pl.multiple_of(target * (stem.shape[2] // group), chunk), chunk)
    copies = []
    for i in range(local_a // ROWS):
        rows = slice(i * ROWS, (i + 1) * ROWS)
        copies.append(
            pltpu.make_async_copy(stem.at[:, rows, columns], held.at[:, rows], sems.at[i])
        )
        copies[-1].start()
    for i, copy in enumerate(copies):
        copy.wait()
        for c in range(2):
            for h in range(width // 128):
                lanes = slice(h * 128, (h + 1) * 128)
                for a in range(ROWS):
                    turned[c, h, pl.ds(a, chunk, stride=ROWS), :] = held[
                        c, i * ROWS + a, :, lanes
                    ].astype(jnp.float32)
                out[c, :, i * ROWS : (i + 1) * ROWS, lanes] = (
                    turned[c, h].reshape(chunk, ROWS, 128).astype(jnp.bfloat16)
                )


def first_block(stem, move_turn, group, chunk):
    _, local_a, _, width = stem.shape
    return pl.pallas_call(
        functools.partial(first_block_kernel, move_turn, group),
        in_specs=[pl.BlockSpec(memory_space=pl.ANY)],
        out_specs=pl.BlockSpec(memory_space=pltpu.VMEM),
        out_shape=pltpu.VMEM((2, chunk, local_a, width), jnp.bfloat16),
        scratch_shapes=[
            pltpu.VMEM((2, local_a, chunk, width), jnp.bfloat16),
            pltpu.VMEM((2, width // 128, chunk * ROWS, 128), jnp.float32),
            pltpu.SemaphoreType.DMA((local_a // ROWS,)),
        ],
        compiler_params=pltpu.CompilerParams(vmem_limit_bytes=4 << 20),
        name="first_block",
    )(*placed([stem], pltpu.HBM))


def front_kernel(group, splits, *refs):
    pieces, (w1, w2, close), outs = refs[:group], refs[group : group + 3], refs[group + 3 : -2]
    x, acc = refs[-2:]
    step = pl.program_id(0)
    local_a, width = pieces[0].shape[2:]
    total = group * local_a
    for i, piece in enumerate(pieces):
        for c in range(2):
            x[c * total + i * local_a : c * total + (i + 1) * local_a, :] = piece[c, 0]
    y = jnp.dot(w1[...], x[...], preferred_element_type=jnp.float32)
    lane = lax.broadcasted_iota(jnp.int32, close.shape[1:], 1)

    def column(c):
        return jnp.sum(jnp.where(lane == step, close[c], 0.0), axis=1, keepdims=True)

    cr, ci = column(0), column(1)
    yr, yi = y[:total], y[total:]
    phased = jnp.concatenate(
        [(cr * yr - ci * yi).astype(jnp.bfloat16), (cr * yi + ci * yr).astype(jnp.bfloat16)],
        axis=1,
    )
    both = jnp.dot(phased, w2[...], preferred_element_type=jnp.float32)
    row = lax.rem(step, ROWS)
    for h in range(acc.shape[0]):
        acc[h, pl.ds(row, total, stride=ROWS), :] = both[:, h * 128 : (h + 1) * 128]

    @pl.when(row == ROWS - 1)
    def _():
        first = 0
        for i, out in enumerate(outs):
            count = splits[i % len(splits)]
            for h in range(acc.shape[0]):
                c, lanes = divmod(h * 128, width)
                out[c, :, :, lanes : lanes + 128] = (
                    acc[h, first * ROWS : (first + count) * ROWS, :]
                    .reshape(count, ROWS, 128)
                    .astype(jnp.bfloat16)
                )
            first += count


def front(pieces, w1, w2, close, splits):
    group = len(pieces)
    _, chunk, local_a, width = pieces[0].shape
    total = group * local_a
    return pl.pallas_call(
        functools.partial(front_kernel, group, splits),
        grid=(chunk,),
        in_specs=[pl.BlockSpec((2, 1, local_a, width), lambda b: (0, b, 0, 0))] * group
        + [
            pl.BlockSpec(w1.shape, lambda b: (0, 0)),
            pl.BlockSpec(w2.shape, lambda b: (0, 0)),
            pl.BlockSpec(close.shape, lambda b: (0, 0, 0)),
        ],
        out_specs=[
            pl.BlockSpec((2, count, ROWS, width), lambda b: (0, 0, b // ROWS, 0))
            for count in splits
        ]
        * group,
        out_shape=[pltpu.HBM((2, count, chunk, width), jnp.bfloat16) for count in splits] * group,
        scratch_shapes=[
            pltpu.VMEM((2 * total, width), jnp.bfloat16),
            pltpu.VMEM((2 * width // 128, total * ROWS, 128), jnp.float32),
        ],
        compiler_params=pltpu.CompilerParams(vmem_limit_bytes=40 << 20),
        name="front",
    )(*pieces, w1, w2, close)


def mix_rows(pieces, w3, x, t):
    chunk, _ = pieces[0].shape[2:]
    total = len(pieces) * chunk
    for i, piece in enumerate(pieces):
        for c in range(2):
            x[c * total + i * chunk : c * total + (i + 1) * chunk, :] = piece[c, t]
    return jnp.dot(w3[...], x[...], preferred_element_type=jnp.float32)


def in_place(pieces, counts, body):
    for part, steps in enumerate(counts):

        @pl.loop(0, steps)
        def _(own):
            step = sum(counts[:part]) + own
            rows = pl.ds(step * STEP_ROWS, STEP_ROWS)
            body(part, own, step, [piece.at[:, rows] for piece in pieces])


def in_steps(pieces, buffers, sems, counts, body):
    def copies(step, slot):
        rows = pl.ds(step * STEP_ROWS, STEP_ROWS)
        return [
            pltpu.make_async_copy(piece.at[:, rows], buffers.at[slot, i], sems.at[slot, i])
            for i, piece in enumerate(pieces)
        ]

    for copy in copies(0, 0):
        copy.start()
    for part, steps in enumerate(counts):

        @pl.loop(0, steps)
        def _(own):
            step = sum(counts[:part]) + own
            slot = lax.rem(step, 2)

            @pl.when(step + 1 < sum(counts))
            def _():
                for copy in copies(step + 1, 1 - slot):
                    copy.start()

            for copy in copies(step, slot):
                copy.wait()
            body(part, own, step, [buffers.at[slot, i] for i in range(len(pieces))])


def partial_kernel(n, *refs):
    pieces, w3, outs, (x, buffers, sems) = refs[:n], refs[n], refs[n + 1 : -3], refs[-3:]

    def body(part, own, step, held):
        for t in range(STEP_ROWS):
            outs[part][own * STEP_ROWS + t] = mix_rows(held, w3, x.at[t], t)

    in_steps(pieces, buffers, sems, [out.shape[0] // STEP_ROWS for out in outs], body)


def last_kernel(n, n_bases, start, near, *refs):
    pieces, w3, bases = refs[:n], refs[n], refs[n + 1 : n + 1 + n_bases]
    out, x, held_out, out_sems = refs[-4:] if near else refs[-6:-2]
    counts = [base.shape[0] // STEP_ROWS for base in bases]
    steps = sum(counts)

    def copy_out(step, slot):
        rows = pl.ds(start + step * STEP_ROWS, STEP_ROWS)
        return pltpu.make_async_copy(held_out.at[slot], out.at[rows], out_sems.at[slot])

    def body(part, own, step, held):
        slot = lax.rem(step, 2)

        @pl.when(step >= 2)
        def _():
            copy_out(step - 2, slot).wait()

        for t in range(STEP_ROWS):
            y = bases[part][own * STEP_ROWS + t] + mix_rows(held, w3, x.at[t], t)
            split = y.shape[1] // 128
            for h in range(split):
                lines = pl.ds(h, y.shape[0], stride=split)
                held_out[slot, t, lines, :] = y[:, h * 128 : (h + 1) * 128]
        copy_out(step, slot).start()

    if near:
        in_place(pieces, counts, body)
    else:
        in_steps(pieces, *refs[-2:], counts, body)
    for step in range(max(steps - 2, 0), steps):
        copy_out(step, step % 2).wait()


def placed(pieces, space):
    return [pltpu.with_memory_space_constraint(piece, space) for piece in pieces]


def held_rows(pieces):
    n, (_, _, chunk, width) = len(pieces), pieces[0].shape
    return pltpu.VMEM((STEP_ROWS, 2 * n * chunk, width), jnp.bfloat16)


def copied_rows(pieces):
    n, (_, _, chunk, width) = len(pieces), pieces[0].shape
    return [
        pltpu.VMEM((2, n, 2, STEP_ROWS, chunk, width), jnp.bfloat16),
        pltpu.SemaphoreType.DMA((2, n)),
    ]


def sums_of(count):
    return [min(SUM_ROWS, count - first) for first in range(0, count, SUM_ROWS)]


def partial_b(pieces, w3, sums):
    n, width = len(pieces), pieces[0].shape[3]
    vmem = pl.BlockSpec(memory_space=pltpu.VMEM)
    return pl.pallas_call(
        functools.partial(partial_kernel, n),
        in_specs=[pl.BlockSpec(memory_space=pl.ANY)] * n + [vmem],
        out_specs=[vmem] * len(sums),
        out_shape=[pltpu.VMEM((rows, w3.shape[0], width), jnp.float32) for rows in sums],
        scratch_shapes=[held_rows(pieces)] + copied_rows(pieces),
        compiler_params=pltpu.CompilerParams(vmem_limit_bytes=12 << 20),
        name="partial",
    )(*placed(pieces, pltpu.HBM), w3)


def last_b(pieces, w3, bases, out, start, rows, near):
    width = pieces[0].shape[3]
    n, lines = len(pieces), w3.shape[0] * (width // 128)
    vmem = pl.BlockSpec(memory_space=pltpu.VMEM)
    any_space = pl.BlockSpec(memory_space=pl.ANY)
    given = [] if out is None else [out]
    return pl.pallas_call(
        functools.partial(last_kernel, n, len(bases), start, near),
        in_specs=[vmem if near else any_space] * n
        + [vmem] * (1 + len(bases))
        + [any_space] * len(given),
        out_specs=any_space,
        out_shape=jax.ShapeDtypeStruct((rows, lines, 128), jnp.float32),
        input_output_aliases={n + 1 + len(bases): 0} if given else {},
        scratch_shapes=[
            held_rows(pieces),
            pltpu.VMEM((2, STEP_ROWS, lines, 128), jnp.float32),
            pltpu.SemaphoreType.DMA((2,)),
        ]
        + ([] if near else copied_rows(pieces)),
        compiler_params=pltpu.CompilerParams(vmem_limit_bytes=12 << 20),
        name="last",
    )(
        *placed(pieces, pltpu.VMEM if near else pltpu.HBM),
        w3,
        *placed(bases, pltpu.VMEM),
        *given,
    )


def on_device(stem_tensor, branch_one, branch_two, mode_order, branch_three, closing):
    group = lax.axis_size("inter")
    me = lax.axis_index("inter")
    local_a, width = stem_tensor.shape[1], stem_tensor.shape[4]
    size_b = branch_three.shape[1]
    local_b = size_b // group
    chunk = local_b // B_CHUNKS
    size_a = group * local_a
    if (
        local_b % (B_CHUNKS * 2 * ROWS)
        or local_a % ROWS
        or local_a % STEP_ROWS
        or local_a <= sum(LATE_ROWS)
        or width % 128
        or stem_tensor.shape[3] != 1
    ):
        return small_blocks(stem_tensor, branch_one, branch_two, mode_order, branch_three, closing)

    rounds = rounds_of(group)
    n_rounds = len(rounds)
    place = me.astype(jnp.uint32)
    zero = jnp.uint32(0)
    target = partners(place, rounds, group)
    pairs = [pairs_of(move, turn, group) for move, turn in rounds]

    def send(block, k):
        if k == 0:
            return block
        return lax.ppermute(block, "inter", pairs[k])

    stem = stem_tensor[:, :, :, 0, :]
    arrived = []
    for j in range(B_CHUNKS):
        got = []
        for k in range(n_rounds):
            start = target[k] * jnp.uint32(B_CHUNKS) + jnp.uint32(j)
            ahead = j == 0 and k == 1
            if ahead:
                block = first_block(stem, rounds[k], group, chunk)
            else:
                block = lax.dynamic_slice(
                    stem,
                    (zero, zero, start * jnp.uint32(chunk), zero),
                    (2, local_a, chunk, width),
                    allow_negative_indices=False,
                )
                block = jnp.transpose(block, (0, 2, 1, 3))
            got.append(send(block, k))
        arrived.append(got)

    where_to = jnp.stack(target).astype(jnp.int32)
    where_from = jnp.stack(partners(place, inverse_of(rounds, group), group)).astype(jnp.int32)
    one = branch_one.reshape(2, group, local_a, group, local_a)
    one = one[:, where_from][:, :, :, where_to].reshape(2, size_a, size_a)
    one = jnp.transpose(one, (0, 2, 1))
    w1 = jnp.concatenate(
        [
            jnp.concatenate([one[0], -one[1]], axis=1),
            jnp.concatenate([one[1], one[0]], axis=1),
        ],
        axis=0,
    )
    permuted = jnp.zeros_like(branch_two).at[:, mode_order, :].set(branch_two)
    w2 = jnp.concatenate(
        [
            jnp.concatenate([permuted[0], permuted[1]], axis=1),
            jnp.concatenate([-permuted[1], permuted[0]], axis=1),
        ],
        axis=0,
    )
    close = lax.dynamic_slice_in_dim(closing, me * local_b, local_b, 2).astype(jnp.float32)
    close = close.reshape(2, group, local_a, local_b)[:, where_to].reshape(2, size_a, local_b)
    three = branch_three.reshape(2, group, B_CHUNKS, chunk, size_b)[:, where_from]
    three = jnp.transpose(three, (2, 0, 4, 1, 3)).reshape(B_CHUNKS, 2, size_b, group * chunk)
    w3 = [
        jnp.stack(
            [
                jnp.concatenate([part[0], -part[1]], axis=1),
                jnp.concatenate([part[1], part[0]], axis=1),
            ],
            axis=1,
        ).reshape(2 * size_b, 2 * group * chunk)
        for part in three
    ]
    w1, w2, w3 = lax.optimization_barrier((w1, w2, w3))

    returned = []
    parts = (local_a - sum(LATE_ROWS),) + LATE_ROWS
    for j in range(B_CHUNKS):
        splits = parts if j else (local_a,)
        pieces = front(arrived[j], w1, w2, close[:, :, j * chunk : (j + 1) * chunk], splits)
        for i in range(len(splits)):
            returned.append([send(piece, k) for k, piece in enumerate(pieces[i :: len(splits)])])

    sums = partial_b(returned[0], w3[0], [rows for part in parts for rows in sums_of(part)])
    out, start = None, 0
    for i, count in enumerate(parts):
        own, sums = sums[: len(sums_of(count))], sums[len(sums_of(count)) :]
        out = last_b(returned[1 + i], w3[1], own, out, start, local_a, i > 0)
        start += count
    return out.reshape(local_a, size_b, 2, 1, width)


def solution(mesh):
    in_specs = (P(None, ("cuts", "inter"), None, None, None), P(), P(), P(), P(), P())
    out_specs = P(("cuts", "inter"), None, None, None, None)
    return jax.shard_map(
        on_device, mesh=mesh, in_specs=in_specs, out_specs=out_specs, check_vma=False
    )
```
